256 devices in a mesh: row: 32 (over z_hi, x, core), col: 8 (over z_lo, y).
Axes of the slice: x: 4, y: 4, z: 8 (z_hi: 4, z_lo: 2; z = z_hi * 2 + z_lo), core: 2. Of those that a mesh axis runs over, the one named last changes fastest.
Arguments:
- blocks: bfloat16 [32, 512, 128, 128], P('row', 'col')
- block_rows: int32 [32, 512], P('row', 'col'), may hold values from 0 to 255, as said below
- block_cols: int32 [32, 512], P('row', 'col'), may hold values from 0 to 255, as said below
- counts: int32 [32, 8], P('row', 'col'), may hold values from 1 to 64, as said below
- trials: bfloat16 [32768, 256], P(('col', 'row')), may hold values from -6 to 6
Outputs:
- basis: float32 [32768, 256], P(('col', 'row'))
- factor: float32 [256, 256], replicated
The draws below stay inside these ranges and needn't reach their ends.
Inputs may be any that keep to these rules, and one draw needn't show every extreme that they name: The live slots of a device are its first counts[r, c] slots, and at least one device has all 64 slots live. `block_rows`: for the device at grid position (r, c), every slot's block row leaves remainder r on division by the size of axis row. The live slots of a device name distinct blocks with block row at most block column; slots past the count hold arbitrary blocks whose coordinates have the same form. `block_cols`: for the device at grid position (r, c), every slot's block column divided by the size of axis row gives c.
All inputs are finite; a program needn't handle non-finite values.
Results may differ from the reference program's by a relative error of at most 0.0003.
Values may be sent and summed in bfloat16 or wider, within the bound.
No kernel may reach another device: no remote copies, remote signals or barrier semaphores. Data moves between devices by JAX's collectives and lax.ppermute only.
A program may use at most 64 MiB of HBM per device.

```python
import jax
import jax.numpy as jnp
from jax import lax

BS = 128
K = 256
SLOTS = 64
NW = 32768
N_ROW = 32
N_COL = 8


def block_layout(key):
    base_key = jax.random.fold_in(key, 4021)
    score_key, load_key, pick_key = jax.random.split(base_key, 3)
    tile_size = N_ROW * N_COL
    grid_row = jnp.arange(N_ROW, dtype=jnp.int32)[:, None, None]
    grid_col = jnp.arange(N_COL, dtype=jnp.int32)[None, :, None]
    places = jnp.arange(tile_size, dtype=jnp.int32)[None, None, :]
    row_index = places // N_ROW * N_ROW + grid_row
    col_index = grid_col * N_ROW + places % N_ROW
    allowed = row_index <= col_index
    scores = jax.random.randint(score_key, (N_ROW, N_COL, tile_size), 0, 1 << 20) * tile_size + places
    scores = jnp.where(allowed, scores, scores + (1 << 29))
    order = jnp.argsort(scores, axis=-1)[:, :, :SLOTS].astype(jnp.int32)
    row_full = jnp.broadcast_to(row_index, scores.shape)
    col_full = jnp.broadcast_to(col_index, scores.shape)
    row_pick = jnp.take_along_axis(row_full, order, axis=-1)
    col_pick = jnp.take_along_axis(col_full, order, axis=-1)
    room = grid_col[:, :, 0] * N_ROW + N_ROW - grid_row[:, :, 0]
    loads = jax.random.randint(load_key, (N_ROW, N_COL), 1, 2 * SLOTS // 3 + 1)
    loads = jnp.minimum(loads, room)
    full_row = jax.random.randint(pick_key, (), 0, min(N_ROW, N_ROW * N_COL - SLOTS + 1))
    forced = (jnp.arange(N_ROW, dtype=jnp.int32)[:, None] == full_row) & (jnp.arange(N_COL, dtype=jnp.int32)[None, :] == N_COL - 1)
    loads = jnp.where(forced, SLOTS, loads).astype(jnp.int32)
    return (row_pick.reshape(N_ROW, N_COL * SLOTS), col_pick.reshape(N_ROW, N_COL * SLOTS), loads)


def draw_block_rows(key, part):
    return block_layout(key)[0]


def draw_block_cols(key, part):
    return block_layout(key)[1]


def draw_counts(key, part):
    return block_layout(key)[2]


def draw_blocks(key, part):
    row_pick, col_pick, loads = block_layout(key)
    base_key, rough_key = jax.random.split(jax.random.fold_in(key, 977), 2)
    shape = (N_ROW, N_COL * SLOTS, BS, BS)
    base = jax.random.normal(base_key, shape, jnp.float32)
    places = jnp.arange(N_ROW * N_COL, dtype=jnp.int32)
    rough = jnp.exp(jax.random.uniform(rough_key, (N_ROW * N_COL,), jnp.float32, -0.69, 0.69))
    profile = jnp.exp(0.55 * (2.0 * (places % N_ROW).astype(jnp.float32) / (N_ROW - 1) - 1.0)) * rough
    amplitude = profile[row_pick] * profile[col_pick]
    return (base * amplitude[:, :, None, None] * (BS * SLOTS) ** (-0.5)).astype(jnp.bfloat16)


def block_levels(key, dims, cuts, low, high):
    level, own = 1.0, jax.random.fold_in(key, 6)
    for position, shards_of in cuts:
        steps = jnp.exp(jax.random.uniform(jax.random.fold_in(own, position), (shards_of,), jnp.float32, low / len(cuts), high / len(cuts)))
        level = level * jnp.repeat(steps, dims[position] // shards_of).reshape([-1 if axis == position else 1 for axis in range(len(dims))])
    return level


def bell_draw(rng, extent, spread, bound, cuts=(), kind=jnp.bfloat16):
    drawn = jax.random.normal(rng, extent, jnp.float32) * spread
    if len(cuts) > 0:
        drawn = block_levels(rng, extent, cuts, -0.22, 0.18) * drawn
    return jnp.clip(drawn, min=-bound, max=bound).astype(kind)


def setup_inputs(seed: int = 0) -> dict:
    key_of = jax.random.split(jax.random.key(seed), 6)
    return {
        "blocks": draw_blocks(jax.random.fold_in(key_of[5], 71), 0),
        "block_rows": draw_block_rows(jax.random.fold_in(key_of[5], 71), 0),
        "block_cols": draw_block_cols(jax.random.fold_in(key_of[5], 71), 0),
        "counts": draw_counts(jax.random.fold_in(key_of[5], 71), 0),
        "trials": bell_draw(key_of[4], (NW, K), 1.0, 6.0, ((0, 256),)),
    }


def reference(blocks, block_rows, block_cols, counts, trials):
    total = N_ROW * N_COL
    flat_blocks = blocks.reshape(total * SLOTS, BS, BS)
    flat_rows = block_rows.reshape(total * SLOTS).astype(jnp.int32)
    flat_cols = block_cols.reshape(total * SLOTS).astype(jnp.int32)
    positions = jnp.arange(SLOTS, dtype=jnp.int32)[None, None, :]
    alive = (positions < counts[:, :, None]).reshape(total * SLOTS)
    weights = jnp.where(alive, jnp.where(flat_rows == flat_cols, 0.5, 1.0), 0.0).astype(jnp.float32)
    vectors = trials.reshape(total, BS, K)

    def add_block(accum, item):
        tile, row_at, col_at, weight = item

        def apply_block(inner):
            direct = jnp.dot(tile.astype(jnp.float32), vectors[col_at].astype(jnp.float32), preferred_element_type=jnp.float32)
            mirror = jnp.dot(tile.T.astype(jnp.float32), vectors[row_at].astype(jnp.float32), preferred_element_type=jnp.float32)
            inner = inner.at[row_at].add(weight * direct)
            return inner.at[col_at].add(weight * mirror)

        def keep_block(inner):
            return inner
        return (lax.cond(weight > 0.0, apply_block, keep_block, accum), None)
    start_value = jnp.zeros((total, BS, K), jnp.float32)
    accum, _ = lax.scan(add_block, start_value, (flat_blocks, flat_rows, flat_cols, weights))
    products = accum.reshape(total * BS, K)
    gram = jnp.dot(products.T.astype(jnp.float32), products.astype(jnp.float32), precision=lax.Precision.HIGHEST, preferred_element_type=jnp.float32) / (total * BS)
    lower = jnp.linalg.cholesky(gram)
    basis = jax.scipy.linalg.solve_triangular(lower, products.T, lower=True).T
    return (basis, lower.T)
```

```python
import jax
import jax.numpy as jnp
from jax import lax
from jax.experimental import pallas as pl
from jax.experimental.pallas import tpu as pltpu
from jax.sharding import PartitionSpec as P


N_ZH, N_X, N_CORE, N_ZL, N_Y = 4, 4, 2, 2, 4
N_ROW = N_ZH * N_X * N_CORE
N_COL = N_ZL * N_Y
F32 = jnp.float32


def row_at(z, x, c):
    return ((z % N_ZH) * N_X + x % N_X) * N_CORE + c


def col_at(zl, y):
    return zl * N_Y + y % N_Y


def row_pairs(move):
    return [(row_at(z, x, c), row_at(*move(z, x, c))) for z in range(N_ZH) for x in range(N_X) for c in range(N_CORE)]


def to_z(v, k):
    return lax.ppermute(v, "row", row_pairs(lambda z, x, c: (z + k, x, c)))


def to_x(v, k):
    return lax.ppermute(v, "row", row_pairs(lambda z, x, c: (z, x + k, c)))


def to_core(v):
    return lax.ppermute(v, "row", row_pairs(lambda z, x, c: (z, x, 1 - c)))


def to_y(v, k):
    return lax.ppermute(v, "col", [(col_at(zl, y), col_at(zl, y + k)) for zl in range(N_ZL) for y in range(N_Y)])


def to_zl(v):
    return lax.ppermute(v, "col", [(col_at(zl, y), col_at(1 - zl, y)) for zl in range(N_ZL) for y in range(N_Y)])


def ring_sum(parts):
    return (parts[0] + parts[2]) + (parts[1] + parts[3])


def sweep_kernel(place, counts, rows, cols, blocks, row_vectors, col_vectors, *refs):
    row_outs, col_outs, row_acc, col_acc = refs[:4], refs[4:6], refs[6], refs[7]
    r, c = place[0], place[1]
    my_z, my_x, my_core = r // (N_X * N_CORE), (r // N_CORE) % N_X, r % N_CORE
    my_zl, my_y = c // N_Y, c % N_Y
    live = counts[0, 0]
    row_acc[...] = jnp.zeros_like(row_acc)
    col_acc[...] = jnp.zeros_like(col_acc)

    def visit(s):
        i, j = rows[0, s], cols[0, s]
        rp, cp = i // N_ROW, j % N_ROW
        yk, zlx = (rp % N_Y - my_y) % N_Y, (rp // N_Y + my_zl) % N_ZL
        zk = (cp // (N_X * N_CORE) - my_z) % N_ZH
        xk = ((cp // N_CORE) % N_X - my_x) % N_X
        cx = (cp % N_CORE + my_core) % N_CORE
        q = jnp.where(s < live, jnp.where(i == j, 0.5, 1.0), 0.0)
        tile = blocks[s].astype(F32)
        tile = jnp.where(q > 0.0, tile * q, 0.0).astype(jnp.bfloat16)
        rpos, cpos = yk * N_ZL + zlx, (cx * N_X + xk) * N_ZH + zk
        row_acc[rpos] += jnp.dot(tile, col_vectors[cpos], preferred_element_type=F32)
        col_acc[cpos] += lax.dot_general(
            tile, row_vectors[rpos], (((0,), (0,)), ((), ())), preferred_element_type=F32
        )

    def group(g, carry):
        for u in range(4):
            visit(g * 4 + u)
        return carry

    lax.fori_loop(0, (live + 3) // 4, group, 0)
    for k in range(N_Y):
        row_outs[k][...] = row_acc[k * N_ZL : (k + 1) * N_ZL]
    for k in range(N_CORE):
        col_outs[k][...] = col_acc[k * N_X * N_ZH : (k + 1) * N_X * N_ZH]


def sweep(place, counts, rows, cols, blocks, row_vectors, col_vectors):
    edge, width = row_vectors.shape[1:]
    smem = pl.BlockSpec(memory_space=pltpu.SMEM)
    vmem = pl.BlockSpec(memory_space=pltpu.VMEM)
    row_out = jax.ShapeDtypeStruct((N_ZL, edge, width), F32)
    col_out = jax.ShapeDtypeStruct((N_X * N_ZH, edge, width), F32)
    return pl.pallas_call(
        sweep_kernel,
        out_shape=(row_out,) * N_Y + (col_out,) * N_CORE,
        in_specs=[smem] * 4 + [vmem] * 3,
        out_specs=(vmem,) * (N_Y + N_CORE),
        scratch_shapes=[
            pltpu.VMEM((N_COL, edge, width), F32),
            pltpu.VMEM((N_ROW, edge, width), F32),
        ],
        name="sweep",
    )(place, counts, rows, cols, blocks, row_vectors, col_vectors)


def gram_total(products, place):
    width = products.shape[1]
    half, piece = width // N_CORE, width // (N_CORE * N_Y)
    r, c = place[0], place[1]
    my_core, my_y = r % N_CORE, c % N_Y
    local = jnp.dot(products.T, products, precision=lax.Precision.HIGHEST, preferred_element_type=F32)
    mine = lax.dynamic_slice_in_dim(local, my_core * half, half, 0)
    other = lax.dynamic_slice_in_dim(local, (1 - my_core) * half, half, 0)
    pair = mine + to_core(other)
    parts = [lax.dynamic_slice_in_dim(pair, ((my_y + k) % N_Y) * piece, piece, 0) for k in range(N_Y)]
    got = ring_sum([parts[0]] + [to_y(parts[k], k) for k in range(1, N_Y)])
    got = ring_sum([got] + [to_x(got, k) for k in range(1, N_X)])
    got = got + to_zl(got)
    got = ring_sum([got] + [to_z(got, k) for k in range(1, N_ZH)])
    ring = [got] + [to_y(got, -k) for k in range(1, N_Y)]
    doubled = jnp.concatenate(ring + ring, 0)
    mine = lax.dynamic_slice_in_dim(doubled, ((N_Y - my_y) % N_Y) * piece, half, 0)
    other = to_core(mine)
    pair = jnp.concatenate([mine, other, mine], 0)
    return lax.dynamic_slice_in_dim(pair, my_core * half, width, 0)


def body(blocks, block_rows, block_cols, counts, trials):
    edge, width = trials.shape
    place = jnp.stack([lax.axis_index("row"), lax.axis_index("col")]).astype(jnp.int32)
    first = jnp.stack([trials, to_zl(trials)])
    row_vectors = jnp.concatenate([first] + [to_y(first, -k) for k in range(1, N_Y)], 0)
    zs = jnp.stack([trials] + [to_z(trials, -k) for k in range(1, N_ZH)])
    xs = jnp.concatenate([zs] + [to_x(zs, -k) for k in range(1, N_X)], 0)
    col_vectors = jnp.concatenate([xs, to_core(xs)], 0)
    outs = sweep(place, counts, block_rows, block_cols, blocks[0], row_vectors, col_vectors)
    row_outs, (col_keep, col_send) = outs[:N_Y], outs[N_Y:]
    pair = col_keep + to_core(col_send)
    parts = [pair[k * N_ZH : (k + 1) * N_ZH] for k in range(N_X)]
    rows = ring_sum([row_outs[0]] + [to_y(row_outs[k], k) for k in range(1, N_Y)])
    got = ring_sum([parts[0]] + [to_x(parts[k], k) for k in range(1, N_X)])
    row_sum = rows[0] + to_zl(rows[1])
    col_sum = ring_sum([got[0]] + [to_z(got[k], k) for k in range(1, N_ZH)])
    products = row_sum + col_sum
    gram = gram_total(products, place) / (N_ROW * N_COL * edge)
    lower = jnp.linalg.cholesky(gram)
    basis = jax.scipy.linalg.solve_triangular(lower, products.T, lower=True).T
    return (basis, lower.T)


def solution(mesh):
    return jax.shard_map(
        body,
        mesh=mesh,
        in_specs=(
            P("row", "col", None, None),
            P("row", "col"),
            P("row", "col"),
            P("row", "col"),
            P(("col", "row"), None),
        ),
        out_specs=(P(("col", "row"), None), P()),
        check_vma=False,
    )
```

```python
import jax
import jax.numpy as jnp
from jax import lax
from jax.experimental import pallas as pl
from jax.experimental.pallas import tpu as pltpu
from jax.sharding import PartitionSpec as P


N_ZH, N_X, N_CORE, N_ZL, N_Y = 4, 4, 2, 2, 4
N_ROW = N_ZH * N_X * N_CORE
N_COL = N_ZL * N_Y
F32 = jnp.float32
BLOCK, STEP, SUB, LANES = 64, 4, 8, 128


def row_at(z, x, c):
    return ((z % N_ZH) * N_X + x % N_X) * N_CORE + c


def col_at(zl, y):
    return zl * N_Y + y % N_Y


def row_pairs(move):
    return [(row_at(z, x, c), row_at(*move(z, x, c))) for z in range(N_ZH) for x in range(N_X) for c in range(N_CORE)]


def to_z(v, k):
    return lax.ppermute(v, "row", row_pairs(lambda z, x, c: (z + k, x, c)))


def to_x(v, k):
    return lax.ppermute(v, "row", row_pairs(lambda z, x, c: (z, x + k, c)))


def to_core(v):
    return lax.ppermute(v, "row", row_pairs(lambda z, x, c: (z, x, 1 - c)))


def to_y(v, k):
    return lax.ppermute(v, "col", [(col_at(zl, y), col_at(zl, y + k)) for zl in range(N_ZL) for y in range(N_Y)])


def to_zl(v):
    return lax.ppermute(v, "col", [(col_at(zl, y), col_at(1 - zl, y)) for zl in range(N_ZL) for y in range(N_Y)])


def ring_sum(parts):
    return (parts[0] + parts[2]) + (parts[1] + parts[3])


def sweep_kernel(place, counts, rows, cols, blocks, row_vectors, col_vectors, *refs):
    row_outs, col_outs, row_acc, col_acc = refs[:4], refs[4:6], refs[6], refs[7]
    r, c = place[0], place[1]
    my_z, my_x, my_core = r >> 3, (r >> 1) & 3, r & 1
    my_zl, my_y = c >> 2, c & 3
    live = counts[0, 0]
    row_acc[...] = jnp.zeros_like(row_acc)
    col_acc[...] = jnp.zeros_like(col_acc)

    def visit(s):
        i, j = rows[0, s], cols[0, s]
        rp, cp = i >> 5, j & (N_ROW - 1)
        yk, zlx = ((rp & 3) - my_y) & 3, (rp >> 2) ^ my_zl
        zk, xk, cx = ((cp >> 3) - my_z) & 3, (((cp >> 1) & 3) - my_x) & 3, (cp & 1) ^ my_core
        q = jnp.where(s < live, jnp.where(i == j, 0.5, 1.0), 0.0)
        tile = blocks[s].astype(F32)
        tile = jnp.where(q > 0.0, tile * q, 0.0).astype(jnp.bfloat16)
        rpos, cpos = yk * N_ZL + zlx, (cx * N_X + xk) * N_ZH + zk
        row_acc[rpos] += jnp.dot(tile, col_vectors[cpos], preferred_element_type=F32)
        col_acc[cpos] += lax.dot_general(
            tile, row_vectors[rpos], (((0,), (0,)), ((), ())), preferred_element_type=F32
        )

    def group(g, carry):
        for u in range(4):
            visit(g * 4 + u)
        return carry

    lax.fori_loop(0, (live + 3) // 4, group, 0)
    for k in range(N_Y):
        row_outs[k][...] = row_acc[k * N_ZL : (k + 1) * N_ZL]
    for k in range(N_CORE):
        col_outs[k][...] = col_acc[k * N_X * N_ZH : (k + 1) * N_X * N_ZH]


def sweep(place, counts, rows, cols, blocks, row_vectors, col_vectors):
    edge, width = row_vectors.shape[1:]
    smem = pl.BlockSpec(memory_space=pltpu.SMEM)
    vmem = pl.BlockSpec(memory_space=pltpu.VMEM)
    row_out = jax.ShapeDtypeStruct((N_ZL, edge, width), F32)
    col_out = jax.ShapeDtypeStruct((N_X * N_ZH, edge, width), F32)
    return pl.pallas_call(
        sweep_kernel,
        out_shape=(row_out,) * N_Y + (col_out,) * N_CORE,
        in_specs=[smem] * 4 + [vmem] * 3,
        out_specs=(vmem,) * (N_Y + N_CORE),
        scratch_shapes=[
            pltpu.VMEM((N_COL, edge, width), F32),
            pltpu.VMEM((N_ROW, edge, width), F32),
        ],
        name="sweep",
    )(place, counts, rows, cols, blocks, row_vectors, col_vectors)


def spread(v):
    return jnp.broadcast_to(v, (SUB, LANES))


def eliminate(tiles, offset, done):
    below = lax.broadcasted_iota(jnp.int32, (SUB, LANES), 0) >= STEP
    for k in range(0, BLOCK, STEP):
        g, s = divmod(k, SUB)
        lane = offset + k
        head = tiles[g]
        rows = [spread(head[s + a : s + a + 1, :]) for a in range(STEP)]
        pivot = [[spread(head[s + a : s + a + 1, lane + b : lane + b + 1]) for b in range(a + 1)] for a in range(STEP)]
        rest = list(range(g if s == 0 else g + 1, len(tiles)))
        cols = {i: [spread(tiles[i][:, lane + a : lane + a + 1]) for a in range(STEP)] for i in rest}
        inverse = []
        for a in range(STEP):
            inverse.append(1.0 / pivot[a][a])
            for n in range(a + 1, STEP):
                ratio = pivot[n][a] * inverse[a]
                for b in range(a + 1, n + 1):
                    pivot[n][b] = pivot[n][b] - ratio * pivot[b][a]
                rows[n] = rows[n] - ratio * rows[a]
                for i in rest:
                    cols[i][n] = cols[i][n] - ratio * cols[i][a]
        for a in range(STEP):
            done[k + a : k + a + 1, :] = (rows[a] * lax.rsqrt(pivot[a][a]))[0:1, :]
        scaled = [rows[a] * inverse[a] for a in range(STEP)]
        for i in rest:
            take = (cols[i][0] * scaled[0] + cols[i][1] * scaled[1]) + (cols[i][2] * scaled[2] + cols[i][3] * scaled[3])
            if i == g:
                take = jnp.where(below, take, 0.0)
            tiles[i] = tiles[i] - take


def factor_kernel(place, piece0, piece1, piece2, piece3, products, basis, factor, work, done):
    edge, size = products.shape
    rows = size // (N_CORE * N_Y)
    my_core, my_y = place[0] & (N_CORE - 1), place[1] & (N_Y - 1)
    for k, piece in enumerate((piece0, piece1, piece2, piece3)):
        for side in range(N_CORE):
            at = (((my_core + side) & 1) * N_Y + ((my_y + k) & (N_Y - 1))) * rows
            work[pl.ds(pl.multiple_of(at, rows), rows), :size] = piece[side] * (1.0 / (N_ROW * N_COL * edge))
    work[:, size:] = products[...].T
    for p in range(size // BLOCK):
        top = p * BLOCK
        tile, offset = top // LANES * LANES, top % LANES
        lanes = lax.broadcasted_iota(jnp.int32, (SUB, LANES), 1)
        subs = lax.broadcasted_iota(jnp.int32, (SUB, LANES), 0)
        inside = (lanes >= offset) & (lanes < offset + BLOCK)
        tiles = []
        for i in range(BLOCK // SUB):
            unit = jnp.where(lanes == subs + (i * SUB + BLOCK - offset), 1.0, 0.0)
            part = work[top + i * SUB : top + (i + 1) * SUB, tile : tile + LANES]
            tiles.append(jnp.where(inside, part, unit))
        eliminate(tiles, offset, done)
        inside_all = lax.broadcasted_iota(jnp.int32, (BLOCK, LANES), 1) // BLOCK == offset // BLOCK
        inverse = jnp.where(inside_all, 0.0, done[...])
        panel = work[top : top + BLOCK, :]
        upper = jnp.dot(inverse, jnp.concatenate([panel, panel], 0), precision=lax.Precision.HIGHEST, preferred_element_type=F32)
        rows = lax.broadcasted_iota(jnp.int32, (BLOCK, size), 0) + top
        keep = lax.broadcasted_iota(jnp.int32, (BLOCK, size), 1) >= rows
        head = jnp.where(keep, upper[:, :size], 0.0)
        factor[top : top + BLOCK, :] = head
        work[top : top + BLOCK, size:] = upper[:, size:]
        if top + BLOCK < size:
            low = (top + BLOCK) // LANES * LANES
            full = jnp.concatenate([head, upper[:, size:]], 1)
            take = lax.dot_general(
                head[:, low:], full[:, low:], (((0,), (0,)), ((), ())), precision=lax.Precision.HIGHEST, preferred_element_type=F32
            )
            work[top + BLOCK :, low:] = work[top + BLOCK :, low:] - take[top + BLOCK - low :, :]
    basis[...] = work[:, size:].T


def factor_and_basis(place, pieces, products):
    edge, size = products.shape
    vmem = pl.BlockSpec(memory_space=pltpu.VMEM)
    return pl.pallas_call(
        factor_kernel,
        out_shape=(jax.ShapeDtypeStruct((edge, size), F32), jax.ShapeDtypeStruct((size, size), F32)),
        in_specs=[pl.BlockSpec(memory_space=pltpu.SMEM)] + [vmem] * 5,
        out_specs=(vmem, vmem),
        scratch_shapes=[pltpu.VMEM((size, size + edge), F32), pltpu.VMEM((BLOCK, LANES), F32)],
        name="factor",
    )(place, *pieces, products)


def gram_pieces(products, place):
    width = products.shape[1]
    half, piece = width // N_CORE, width // (N_CORE * N_Y)
    my_core, my_y = place[0] & (N_CORE - 1), place[1] & (N_Y - 1)
    local = jnp.dot(products.T, products, precision=lax.Precision.HIGHEST, preferred_element_type=F32)
    mine = lax.dynamic_slice_in_dim(local, my_core * half, half, 0)
    other = lax.dynamic_slice_in_dim(local, (1 - my_core) * half, half, 0)
    pair = mine + to_core(other)
    parts = [lax.dynamic_slice_in_dim(pair, ((my_y + k) & (N_Y - 1)) * piece, piece, 0) for k in range(N_Y)]
    got = ring_sum([parts[0]] + [to_y(parts[k], k) for k in range(1, N_Y)])
    got = ring_sum([got] + [to_x(got, k) for k in range(1, N_X)])
    got = got + to_zl(got)
    got = ring_sum([got] + [to_z(got, k) for k in range(1, N_ZH)])
    both = jnp.stack([got, to_core(got)])
    return [both] + [to_y(both, -k) for k in range(1, N_Y)]


def body(blocks, block_rows, block_cols, counts, trials):
    edge, width = trials.shape
    place = jnp.stack([lax.axis_index("row"), lax.axis_index("col")]).astype(jnp.int32)
    first = jnp.stack([trials, to_zl(trials)])
    zs = jnp.stack([trials] + [to_z(trials, -k) for k in range(1, N_ZH)])
    first, zs = lax.optimization_barrier((first, zs))
    row_vectors = jnp.concatenate([first] + [to_y(first, -k) for k in range(1, N_Y)], 0)
    xs = jnp.concatenate([zs] + [to_x(zs, -k) for k in range(1, N_X)], 0)
    row_vectors, xs = lax.optimization_barrier((row_vectors, xs))
    col_vectors = jnp.concatenate([xs, to_core(xs)], 0)
    outs = sweep(place, counts, block_rows, block_cols, blocks[0], row_vectors, col_vectors)
    row_outs, (col_keep, col_send) = outs[:N_Y], outs[N_Y:]
    pair = col_keep + to_core(col_send)
    parts = [pair[k * N_ZH : (k + 1) * N_ZH] for k in range(N_X)]
    rows = ring_sum([row_outs[0]] + [to_y(row_outs[k], k) for k in range(1, N_Y)])
    got = ring_sum([parts[0]] + [to_x(parts[k], k) for k in range(1, N_X)])
    row_sum = rows[0] + to_zl(rows[1])
    col_sum = ring_sum([got[0]] + [to_z(got[k], k) for k in range(1, N_ZH)])
    products = row_sum + col_sum
    return factor_and_basis(place, gram_pieces(products, place), products)


def solution(mesh):
    return jax.shard_map(
        body,
        mesh=mesh,
        in_specs=(
            P("row", "col", None, None),
            P("row", "col"),
            P("row", "col"),
            P("row", "col"),
            P(("col", "row"), None),
        ),
        out_specs=(P(("col", "row"), None), P()),
        check_vma=False,
    )
```

```python
import jax
import jax.numpy as jnp
from jax import lax
from jax.experimental import pallas as pl
from jax.experimental.pallas import tpu as pltpu
from jax.sharding import PartitionSpec as P


N_ZH, N_X, N_CORE, N_ZL, N_Y = 4, 4, 2, 2, 4
N_ROW = N_ZH * N_X * N_CORE
N_COL = N_ZL * N_Y
F32 = jnp.float32
BLOCK, STEP, SUB, LANES = 64, 4, 8, 128


def row_at(z, x, c):
    return ((z % N_ZH) * N_X + x % N_X) * N_CORE + c


def col_at(zl, y):
    return zl * N_Y + y % N_Y


def row_pairs(move):
    return [(row_at(z, x, c), row_at(*move(z, x, c))) for z in range(N_ZH) for x in range(N_X) for c in range(N_CORE)]


def to_z(v, k):
    return lax.ppermute(v, "row", row_pairs(lambda z, x, c: (z + k, x, c)))


def to_x(v, k):
    return lax.ppermute(v, "row", row_pairs(lambda z, x, c: (z, x + k, c)))


def to_core(v):
    return lax.ppermute(v, "row", row_pairs(lambda z, x, c: (z, x, 1 - c)))


def to_y(v, k):
    return lax.ppermute(v, "col", [(col_at(zl, y), col_at(zl, y + k)) for zl in range(N_ZL) for y in range(N_Y)])


def to_zl(v):
    return lax.ppermute(v, "col", [(col_at(zl, y), col_at(1 - zl, y)) for zl in range(N_ZL) for y in range(N_Y)])


def ring_sum(parts):
    return (parts[0] + parts[2]) + (parts[1] + parts[3])


def slot_loop(counts, rows, cols, blocks, add):
    live = counts[0, 0]

    def visit(s):
        i, j = rows[0, s], cols[0, s]
        q = jnp.where(s < live, jnp.where(i == j, 0.5, 1.0), 0.0)
        tile = jnp.where(q > 0.0, blocks[s].astype(F32) * q, 0.0).astype(jnp.bfloat16)
        add(tile, i >> 5, j & (N_ROW - 1))

    def group(g, carry):
        for u in range(4):
            visit(g * 4 + u)
        return carry

    lax.fori_loop(0, (live + 3) // 4, group, 0)


def row_spot(place, rp):
    return ((rp - place[1]) & 3) * N_ZL + ((rp >> 2) ^ (place[1] >> 2))


def col_spot(place, cp):
    r = place[0]
    zk, xk, cx = ((cp >> 3) - (r >> 3)) & 3, ((cp >> 1) - (r >> 1)) & 3, (cp ^ r) & 1
    return (cx * N_X + xk) * N_ZH + zk


def mirror_kernel(place, counts, rows, cols, blocks, *refs):
    pieces, outs, vectors, acc = refs[:N_Y], refs[N_Y : N_Y + N_CORE], refs[-2], refs[-1]
    acc[...] = jnp.zeros_like(acc)
    for k, piece in enumerate(pieces):
        vectors[k * N_ZL : (k + 1) * N_ZL] = piece[...]

    def add(tile, rp, cp):
        acc[col_spot(place, cp)] += lax.dot_general(
            tile, vectors[row_spot(place, rp)], (((0,), (0,)), ((), ())), preferred_element_type=F32
        )

    slot_loop(counts, rows, cols, blocks, add)
    for k, out in enumerate(outs):
        out[...] = acc[k * N_X * N_ZH : (k + 1) * N_X * N_ZH]


def direct_kernel(place, counts, rows, cols, blocks, *refs):
    n = N_CORE * N_X
    pieces, outs, vectors, acc = refs[:n], refs[n : n + N_Y], refs[-2], refs[-1]
    acc[...] = jnp.zeros_like(acc)
    for k, piece in enumerate(pieces):
        vectors[k * N_ZH : (k + 1) * N_ZH] = piece[...]

    def add(tile, rp, cp):
        acc[row_spot(place, rp)] += jnp.dot(tile, vectors[col_spot(place, cp)], preferred_element_type=F32)

    slot_loop(counts, rows, cols, blocks, add)
    for k, out in enumerate(outs):
        out[...] = acc[k * N_ZL : (k + 1) * N_ZL]


def products_of(kernel, scalars, blocks, pieces, n_out, out_blocks):
    edge, width = pieces[0].shape[1:]
    smem = pl.BlockSpec(memory_space=pltpu.SMEM)
    vmem = pl.BlockSpec(memory_space=pltpu.VMEM)
    n_in = len(pieces) * pieces[0].shape[0]
    return pl.pallas_call(
        kernel,
        out_shape=(jax.ShapeDtypeStruct((out_blocks, edge, width), F32),) * n_out,
        in_specs=[smem] * 4 + [vmem] * (1 + len(pieces)),
        out_specs=(vmem,) * n_out,
        scratch_shapes=[
            pltpu.VMEM((n_in, edge, width), jnp.bfloat16),
            pltpu.VMEM((n_out * out_blocks, edge, width), F32),
        ],
        cost_estimate=pl.CostEstimate(
            flops=2 * blocks.shape[0] * edge * edge * width,
            bytes_accessed=2 * blocks.size + 2 * n_in * edge * width + 4 * n_out * out_blocks * edge * width,
            transcendentals=0,
        ),
    )(*scalars, blocks, *pieces)


def spread(v):
    return jnp.broadcast_to(v, (SUB, LANES))


def eliminate(tiles, offset, done):
    below = lax.broadcasted_iota(jnp.int32, (SUB, LANES), 0) >= STEP
    for k in range(0, BLOCK, STEP):
        g, s = divmod(k, SUB)
        lane = offset + k
        head = tiles[g]
        rows = [spread(head[s + a : s + a + 1, :]) for a in range(STEP)]
        pivot = [[spread(head[s + a : s + a + 1, lane + b : lane + b + 1]) for b in range(a + 1)] for a in range(STEP)]
        rest = list(range(g if s == 0 else g + 1, len(tiles)))
        cols = {i: [spread(tiles[i][:, lane + a : lane + a + 1]) for a in range(STEP)] for i in rest}
        inverse = []
        for a in range(STEP):
            inverse.append(1.0 / pivot[a][a])
            for n in range(a + 1, STEP):
                ratio = pivot[n][a] * inverse[a]
                for b in range(a + 1, n + 1):
                    pivot[n][b] = pivot[n][b] - ratio * pivot[b][a]
                rows[n] = rows[n] - ratio * rows[a]
                for i in rest:
                    cols[i][n] = cols[i][n] - ratio * cols[i][a]
        for a in range(STEP):
            done[k + a : k + a + 1, :] = (rows[a] * lax.rsqrt(pivot[a][a]))[0:1, :]
        scaled = [rows[a] * inverse[a] for a in range(STEP)]
        for i in rest:
            take = (cols[i][0] * scaled[0] + cols[i][1] * scaled[1]) + (cols[i][2] * scaled[2] + cols[i][3] * scaled[3])
            if i == g:
                take = jnp.where(below, take, 0.0)
            tiles[i] = tiles[i] - take


def factor_kernel(place, piece0, piece1, piece2, piece3, products, basis, factor, work, done):
    edge, size = products.shape
    rows = size // (N_CORE * N_Y)
    my_core, my_y = place[0] & (N_CORE - 1), place[1] & (N_Y - 1)
    for k, piece in enumerate((piece0, piece1, piece2, piece3)):
        for side in range(N_CORE):
            at = (((my_core + side) & 1) * N_Y + ((my_y + k) & (N_Y - 1))) * rows
            work[pl.ds(pl.multiple_of(at, rows), rows), :size] = piece[side] * (1.0 / (N_ROW * N_COL * edge))
    work[:, size:] = products[...].T
    for p in range(size // BLOCK):
        top = p * BLOCK
        tile, offset = top // LANES * LANES, top % LANES
        lanes = lax.broadcasted_iota(jnp.int32, (SUB, LANES), 1)
        subs = lax.broadcasted_iota(jnp.int32, (SUB, LANES), 0)
        inside = (lanes >= offset) & (lanes < offset + BLOCK)
        tiles = []
        for i in range(BLOCK // SUB):
            unit = jnp.where(lanes == subs + (i * SUB + BLOCK - offset), 1.0, 0.0)
            part = work[top + i * SUB : top + (i + 1) * SUB, tile : tile + LANES]
            tiles.append(jnp.where(inside, part, unit))
        eliminate(tiles, offset, done)
        inside_all = lax.broadcasted_iota(jnp.int32, (BLOCK, LANES), 1) // BLOCK == offset // BLOCK
        inverse = jnp.where(inside_all, 0.0, done[...])
        panel = work[top : top + BLOCK, :]
        upper = jnp.dot(inverse, jnp.concatenate([panel, panel], 0), precision=lax.Precision.HIGHEST, preferred_element_type=F32)
        rows = lax.broadcasted_iota(jnp.int32, (BLOCK, size), 0) + top
        keep = lax.broadcasted_iota(jnp.int32, (BLOCK, size), 1) >= rows
        head = jnp.where(keep, upper[:, :size], 0.0)
        factor[top : top + BLOCK, :] = head
        work[top : top + BLOCK, size:] = upper[:, size:]
        if top + BLOCK < size:
            low = (top + BLOCK) // LANES * LANES
            full = jnp.concatenate([head, upper[:, size:]], 1)
            take = lax.dot_general(
                head[:, low:], full[:, low:], (((0,), (0,)), ((), ())), precision=lax.Precision.HIGHEST, preferred_element_type=F32
            )
            work[top + BLOCK :, low:] = work[top + BLOCK :, low:] - take[top + BLOCK - low :, :]
    basis[...] = work[:, size:].T


def factor_and_basis(place, pieces, products):
    edge, size = products.shape
    vmem = pl.BlockSpec(memory_space=pltpu.VMEM)
    return pl.pallas_call(
        factor_kernel,
        out_shape=(jax.ShapeDtypeStruct((edge, size), F32), jax.ShapeDtypeStruct((size, size), F32)),
        in_specs=[pl.BlockSpec(memory_space=pltpu.SMEM)] + [vmem] * 5,
        out_specs=(vmem, vmem),
        scratch_shapes=[pltpu.VMEM((size, size + edge), F32), pltpu.VMEM((BLOCK, LANES), F32)],
        name="factor",
    )(place, *pieces, products)


def gram_pieces(products, place):
    width = products.shape[1]
    half, piece = width // N_CORE, width // (N_CORE * N_Y)
    my_core, my_y = place[0] & (N_CORE - 1), place[1] & (N_Y - 1)
    local = jnp.dot(products.T, products, precision=lax.Precision.HIGHEST, preferred_element_type=F32)
    mine = lax.dynamic_slice_in_dim(local, my_core * half, half, 0)
    other = lax.dynamic_slice_in_dim(local, (1 - my_core) * half, half, 0)
    pair = mine + to_core(other)
    parts = [lax.dynamic_slice_in_dim(pair, ((my_y + k) & (N_Y - 1)) * piece, piece, 0) for k in range(N_Y)]
    got = ring_sum([parts[0]] + [to_y(parts[k], k) for k in range(1, N_Y)])
    got = ring_sum([got] + [to_x(got, k) for k in range(1, N_X)])
    got = got + to_zl(got)
    got = ring_sum([got] + [to_z(got, k) for k in range(1, N_ZH)])
    both = jnp.stack([got, to_core(got)])
    return [both] + [to_y(both, -k) for k in range(1, N_Y)]


def body(blocks, block_rows, block_cols, counts, trials):
    place = jnp.stack([lax.axis_index("row"), lax.axis_index("col")]).astype(jnp.int32)
    scalars = (place, counts, block_rows, block_cols)
    first = jnp.stack([trials, to_zl(trials)])
    zs = jnp.stack([trials] + [to_z(trials, -k) for k in range(1, N_ZH)])
    row_pieces = [first] + [to_y(first, -k) for k in range(1, N_Y)]
    col_pieces = [zs] + [to_x(zs, -k) for k in range(1, N_X)]
    col_keep, col_send = products_of(mirror_kernel, scalars, blocks[0], row_pieces, N_CORE, N_X * N_ZH)
    col_pieces = col_pieces + [to_core(v) for v in col_pieces]
    row_outs = products_of(direct_kernel, scalars, blocks[0], col_pieces, N_Y, N_ZL)
    pair = col_keep + to_core(col_send)
    parts = [pair[k * N_ZH : (k + 1) * N_ZH] for k in range(N_X)]
    got = ring_sum([parts[0]] + [to_x(parts[k], k) for k in range(1, N_X)])
    rows = ring_sum([row_outs[0]] + [to_y(row_outs[k], k) for k in range(1, N_Y)])
    row_sum = rows[0] + to_zl(rows[1])
    col_sum = ring_sum([got[0]] + [to_z(got[k], k) for k in range(1, N_ZH)])
    products = row_sum + col_sum
    return factor_and_basis(place, gram_pieces(products, place), products)


def solution(mesh):
    return jax.shard_map(
        body,
        mesh=mesh,
        in_specs=(
            P("row", "col", None, None),
            P("row", "col"),
            P("row", "col"),
            P("row", "col"),
            P(("col", "row"), None),
        ),
        out_specs=(P(("col", "row"), None), P()),
        check_vma=False,
    )
```

```python
import jax
import jax.numpy as jnp
from jax import lax
from jax.experimental import pallas as pl
from jax.experimental.pallas import tpu as pltpu
from jax.sharding import PartitionSpec as P


N_ZH, N_X, N_CORE, N_ZL, N_Y = 4, 4, 2, 2, 4
N_ROW = N_ZH * N_X * N_CORE
N_COL = N_ZL * N_Y
F32 = jnp.float32
BLOCK, STEP, SUB, LANES = 64, 4, 8, 128


def row_at(z, x, c):
    return ((z % N_ZH) * N_X + x % N_X) * N_CORE + c


def col_at(zl, y):
    return zl * N_Y + y % N_Y


def row_pairs(move):
    return [(row_at(z, x, c), row_at(*move(z, x, c))) for z in range(N_ZH) for x in range(N_X) for c in range(N_CORE)]


def to_z(v, k):
    return lax.ppermute(v, "row", row_pairs(lambda z, x, c: (z + k, x, c)))


def to_x(v, k):
    return lax.ppermute(v, "row", row_pairs(lambda z, x, c: (z, x + k, c)))


def to_core(v):
    return lax.ppermute(v, "row", row_pairs(lambda z, x, c: (z, x, 1 - c)))


def to_y(v, k):
    return lax.ppermute(v, "col", [(col_at(zl, y), col_at(zl, y + k)) for zl in range(N_ZL) for y in range(N_Y)])


def to_zl(v):
    return lax.ppermute(v, "col", [(col_at(zl, y), col_at(1 - zl, y)) for zl in range(N_ZL) for y in range(N_Y)])


def ring_sum(parts):
    return (parts[0] + parts[2]) + (parts[1] + parts[3])


def slot_loop(counts, rows, cols, blocks, add):
    live = counts[0, 0]

    def visit(s):
        i, j = rows[0, s], cols[0, s]
        q = jnp.where(s < live, jnp.where(i == j, 0.5, 1.0), 0.0)
        tile = jnp.where(q > 0.0, blocks[s].astype(F32) * q, 0.0).astype(jnp.bfloat16)
        add(tile, i >> 5, j & (N_ROW - 1))

    def group(g, carry):
        for u in range(4):
            visit(g * 4 + u)
        return carry

    lax.fori_loop(0, (live + 3) // 4, group, 0)


def row_spot(place, rp):
    return ((rp - place[1]) & 3) * N_ZL + ((rp >> 2) ^ (place[1] >> 2))


def col_spot(place, cp):
    r = place[0]
    zk, xk, cx = ((cp >> 3) - (r >> 3)) & 3, ((cp >> 1) - (r >> 1)) & 3, (cp ^ r) & 1
    return (cx * N_X + xk) * N_ZH + zk


def mirror_kernel(place, counts, rows, cols, blocks, *refs):
    vectors, outs, acc = refs[0], refs[1 : 1 + N_CORE], refs[-1]
    acc[...] = jnp.zeros_like(acc)

    def add(tile, rp, cp):
        acc[col_spot(place, cp)] += lax.dot_general(
            tile, vectors[rp], (((0,), (0,)), ((), ())), preferred_element_type=F32
        )

    slot_loop(counts, rows, cols, blocks, add)
    for k, out in enumerate(outs):
        out[...] = acc[k * N_X * N_ZH : (k + 1) * N_X * N_ZH]


def direct_kernel(place, counts, rows, cols, blocks, *refs):
    n = N_CORE * N_X
    pieces, outs, vectors, acc = refs[:n], refs[n : n + N_Y], refs[-2], refs[-1]
    acc[...] = jnp.zeros_like(acc)
    for k, piece in enumerate(pieces):
        vectors[k * N_ZH : (k + 1) * N_ZH] = piece[...]

    def add(tile, rp, cp):
        acc[row_spot(place, rp)] += jnp.dot(tile, vectors[col_spot(place, cp)], preferred_element_type=F32)

    slot_loop(counts, rows, cols, blocks, add)
    for k, out in enumerate(outs):
        out[...] = acc[k * N_ZL : (k + 1) * N_ZL]


def products_of(kernel, scalars, blocks, pieces, n_out, out_blocks):
    edge, width = pieces[0].shape[1:]
    smem = pl.BlockSpec(memory_space=pltpu.SMEM)
    vmem = pl.BlockSpec(memory_space=pltpu.VMEM)
    n_in = len(pieces) * pieces[0].shape[0]
    return pl.pallas_call(
        kernel,
        out_shape=(jax.ShapeDtypeStruct((out_blocks, edge, width), F32),) * n_out,
        in_specs=[smem] * 4 + [vmem] * (1 + len(pieces)),
        out_specs=(vmem,) * n_out,
        scratch_shapes=[
            pltpu.VMEM((n_in, edge, width), jnp.bfloat16),
            pltpu.VMEM((n_out * out_blocks, edge, width), F32),
        ],
        cost_estimate=pl.CostEstimate(
            flops=2 * blocks.shape[0] * edge * edge * width,
            bytes_accessed=2 * blocks.size + 2 * n_in * edge * width + 4 * n_out * out_blocks * edge * width,
            transcendentals=0,
        ),
    )(*scalars, blocks, *pieces)


def spread(v):
    return jnp.broadcast_to(v, (SUB, LANES))


def eliminate(tiles, offset, done):
    below = lax.broadcasted_iota(jnp.int32, (SUB, LANES), 0) >= STEP
    for k in range(0, BLOCK, STEP):
        g, s = divmod(k, SUB)
        lane = offset + k
        head = tiles[g]
        rows = [spread(head[s + a : s + a + 1, :]) for a in range(STEP)]
        pivot = [[spread(head[s + a : s + a + 1, lane + b : lane + b + 1]) for b in range(a + 1)] for a in range(STEP)]
        rest = list(range(g if s == 0 else g + 1, len(tiles)))
        cols = {i: [spread(tiles[i][:, lane + a : lane + a + 1]) for a in range(STEP)] for i in rest}
        inverse = []
        for a in range(STEP):
            inverse.append(1.0 / pivot[a][a])
            for n in range(a + 1, STEP):
                ratio = pivot[n][a] * inverse[a]
                for b in range(a + 1, n + 1):
                    pivot[n][b] = pivot[n][b] - ratio * pivot[b][a]
                rows[n] = rows[n] - ratio * rows[a]
                for i in rest:
                    cols[i][n] = cols[i][n] - ratio * cols[i][a]
        for a in range(STEP):
            done[k + a : k + a + 1, :] = (rows[a] * lax.rsqrt(pivot[a][a]))[0:1, :]
        scaled = [rows[a] * inverse[a] for a in range(STEP)]
        for i in rest:
            take = (cols[i][0] * scaled[0] + cols[i][1] * scaled[1]) + (cols[i][2] * scaled[2] + cols[i][3] * scaled[3])
            if i == g:
                take = jnp.where(below, take, 0.0)
            tiles[i] = tiles[i] - take


def factor_kernel(place, piece0, piece1, piece2, piece3, products, basis, factor, work, done):
    edge, size = products.shape
    rows = size // (N_CORE * N_Y)
    my_core, my_y = place[0] & (N_CORE - 1), place[1] & (N_Y - 1)
    for k, piece in enumerate((piece0, piece1, piece2, piece3)):
        for side in range(N_CORE):
            at = (((my_core + side) & 1) * N_Y + ((my_y + k) & (N_Y - 1))) * rows
            work[pl.ds(pl.multiple_of(at, rows), rows), :size] = piece[side] * (1.0 / (N_ROW * N_COL * edge))
    work[:, size:] = products[...].T
    for p in range(size // BLOCK):
        top = p * BLOCK
        tile, offset = top // LANES * LANES, top % LANES
        lanes = lax.broadcasted_iota(jnp.int32, (SUB, LANES), 1)
        subs = lax.broadcasted_iota(jnp.int32, (SUB, LANES), 0)
        inside = (lanes >= offset) & (lanes < offset + BLOCK)
        tiles = []
        for i in range(BLOCK // SUB):
            unit = jnp.where(lanes == subs + (i * SUB + BLOCK - offset), 1.0, 0.0)
            part = work[top + i * SUB : top + (i + 1) * SUB, tile : tile + LANES]
            tiles.append(jnp.where(inside, part, unit))
        eliminate(tiles, offset, done)
        inside_all = lax.broadcasted_iota(jnp.int32, (BLOCK, LANES), 1) // BLOCK == offset // BLOCK
        inverse = jnp.where(inside_all, 0.0, done[...])
        panel = work[top : top + BLOCK, :]
        upper = jnp.dot(inverse, jnp.concatenate([panel, panel], 0), precision=lax.Precision.HIGHEST, preferred_element_type=F32)
        rows = lax.broadcasted_iota(jnp.int32, (BLOCK, size), 0) + top
        keep = lax.broadcasted_iota(jnp.int32, (BLOCK, size), 1) >= rows
        head = jnp.where(keep, upper[:, :size], 0.0)
        factor[top : top + BLOCK, :] = head
        work[top : top + BLOCK, size:] = upper[:, size:]
        if top + BLOCK < size:
            low = (top + BLOCK) // LANES * LANES
            full = jnp.concatenate([head, upper[:, size:]], 1)
            take = lax.dot_general(
                head[:, low:], full[:, low:], (((0,), (0,)), ((), ())), precision=lax.Precision.HIGHEST, preferred_element_type=F32
            )
            work[top + BLOCK :, low:] = work[top + BLOCK :, low:] - take[top + BLOCK - low :, :]
    basis[...] = work[:, size:].T


def factor_and_basis(place, pieces, products):
    edge, size = products.shape
    vmem = pl.BlockSpec(memory_space=pltpu.VMEM)
    return pl.pallas_call(
        factor_kernel,
        out_shape=(jax.ShapeDtypeStruct((edge, size), F32), jax.ShapeDtypeStruct((size, size), F32)),
        in_specs=[pl.BlockSpec(memory_space=pltpu.SMEM)] + [vmem] * 5,
        out_specs=(vmem, vmem),
        scratch_shapes=[pltpu.VMEM((size, size + edge), F32), pltpu.VMEM((BLOCK, LANES), F32)],
        name="factor",
    )(place, *pieces, products)


def gram_pieces(products, place):
    width = products.shape[1]
    half, piece = width // N_CORE, width // (N_CORE * N_Y)
    my_core, my_y = place[0] & (N_CORE - 1), place[1] & (N_Y - 1)
    local = jnp.dot(products.T, products, precision=lax.Precision.HIGHEST, preferred_element_type=F32)
    mine = lax.dynamic_slice_in_dim(local, my_core * half, half, 0)
    other = lax.dynamic_slice_in_dim(local, (1 - my_core) * half, half, 0)
    pair = mine + to_core(other)
    parts = [lax.dynamic_slice_in_dim(pair, ((my_y + k) & (N_Y - 1)) * piece, piece, 0) for k in range(N_Y)]
    got = ring_sum([parts[0]] + [to_y(parts[k], k) for k in range(1, N_Y)])
    got = ring_sum([got] + [to_x(got, k) for k in range(1, N_X)])
    got = got + to_zl(got)
    got = ring_sum([got] + [to_z(got, k) for k in range(1, N_ZH)])
    both = jnp.stack([got, to_core(got)])
    return [both] + [to_y(both, -k) for k in range(1, N_Y)]


def body(blocks, block_rows, block_cols, counts, trials):
    edge, width = trials.shape
    place = jnp.stack([lax.axis_index("row"), lax.axis_index("col")]).astype(jnp.int32)
    scalars = (place, counts, block_rows, block_cols)
    zs = jnp.stack([trials] + [to_z(trials, -k) for k in range(1, N_ZH)])
    copies = jnp.broadcast_to(trials[None], (N_COL, edge, width))
    row_pieces = [lax.all_to_all(copies, "col", 0, 0, tiled=True)]
    col_pieces = [zs] + [to_x(zs, -k) for k in range(1, N_X)]
    col_keep, col_send = products_of(mirror_kernel, scalars, blocks[0], row_pieces, N_CORE, N_X * N_ZH)
    col_pieces = col_pieces + [to_core(v) for v in col_pieces]
    row_outs = products_of(direct_kernel, scalars, blocks[0], col_pieces, N_Y, N_ZL)
    pair = col_keep + to_core(col_send)
    parts = [pair[k * N_ZH : (k + 1) * N_ZH] for k in range(N_X)]
    got = ring_sum([parts[0]] + [to_x(parts[k], k) for k in range(1, N_X)])
    rows = ring_sum([row_outs[0]] + [to_y(row_outs[k], k) for k in range(1, N_Y)])
    row_sum = rows[0] + to_zl(rows[1])
    col_sum = ring_sum([got[0]] + [to_z(got[k], k) for k in range(1, N_ZH)])
    products = row_sum + col_sum
    return factor_and_basis(place, gram_pieces(products, place), products)


def solution(mesh):
    return jax.shard_map(
        body,
        mesh=mesh,
        in_specs=(
            P("row", "col", None, None),
            P("row", "col"),
            P("row", "col"),
            P("row", "col"),
            P(("col", "row"), None),
        ),
        out_specs=(P(("col", "row"), None), P()),
        check_vma=False,
    )
```

```python
import jax
import jax.numpy as jnp
from jax import lax
from jax.experimental import pallas as pl
from jax.experimental.pallas import tpu as pltpu
from jax.sharding import PartitionSpec as P


N_ZH, N_X, N_CORE, N_ZL, N_Y = 4, 4, 2, 2, 4
N_ROW = N_ZH * N_X * N_CORE
N_COL = N_ZL * N_Y
F32 = jnp.float32
BLOCK, STEP, SUB, LANES = 64, 4, 8, 128


def row_at(z, x, c):
    return ((z % N_ZH) * N_X + x % N_X) * N_CORE + c


def col_at(zl, y):
    return zl * N_Y + y % N_Y


def row_pairs(move):
    return [(row_at(z, x, c), row_at(*move(z, x, c))) for z in range(N_ZH) for x in range(N_X) for c in range(N_CORE)]


def swap_z(v):
    groups = [[row_at(z, x, c) for z in range(N_ZH)] for x in range(N_X) for c in range(N_CORE)]
    return lax.all_to_all(v, "row", 0, 0, tiled=True, axis_index_groups=groups)


def copies(v, n):
    return jnp.broadcast_to(v[None], (n,) + v.shape)


def to_x(v, k):
    return lax.ppermute(v, "row", row_pairs(lambda z, x, c: (z, x + k, c)))


def to_core(v):
    return lax.ppermute(v, "row", row_pairs(lambda z, x, c: (z, x, 1 - c)))


def to_y(v, k):
    return lax.ppermute(v, "col", [(col_at(zl, y), col_at(zl, y + k)) for zl in range(N_ZL) for y in range(N_Y)])


def to_zl(v):
    return lax.ppermute(v, "col", [(col_at(zl, y), col_at(1 - zl, y)) for zl in range(N_ZL) for y in range(N_Y)])


def ring_sum(parts):
    return (parts[0] + parts[2]) + (parts[1] + parts[3])


def slot_loop(counts, rows, cols, blocks, add):
    live = counts[0, 0]

    def visit(s):
        i, j = rows[0, s], cols[0, s]
        q = jnp.where(s < live, jnp.where(i == j, 0.5, 1.0), 0.0)
        tile = jnp.where(q > 0.0, blocks[s].astype(F32) * q, 0.0).astype(jnp.bfloat16)
        add(tile, i >> 5, j & (N_ROW - 1))

    def group(g, carry):
        for u in range(4):
            visit(g * 4 + u)
        return carry

    lax.fori_loop(0, (live + 3) // 4, group, 0)


def row_spot(place, rp):
    return ((rp - place[1]) & 3) * N_ZL + ((rp >> 2) ^ (place[1] >> 2))


def col_spot(place, cp):
    r = place[0]
    z, xk, cx = cp >> 3, ((cp >> 1) - (r >> 1)) & 3, (cp ^ r) & 1
    return (cx * N_X + xk) * N_ZH + z


def mirror_kernel(place, counts, rows, cols, blocks, *refs):
    pieces, outs, vectors, acc = refs[:N_Y], refs[N_Y : N_Y + N_CORE], refs[-2], refs[-1]
    acc[...] = jnp.zeros_like(acc)
    for k, piece in enumerate(pieces):
        vectors[k * N_ZL : (k + 1) * N_ZL] = piece[...]

    def add(tile, rp, cp):
        acc[col_spot(place, cp)] += lax.dot_general(
            tile, vectors[row_spot(place, rp)], (((0,), (0,)), ((), ())), preferred_element_type=F32
        )

    slot_loop(counts, rows, cols, blocks, add)
    for k, out in enumerate(outs):
        out[...] = acc[k * N_X * N_ZH : (k + 1) * N_X * N_ZH]


def direct_kernel(place, counts, rows, cols, blocks, *refs):
    n = N_CORE * N_X
    pieces, acc, vectors = refs[:n], refs[n], refs[n + 1]
    acc[...] = jnp.zeros_like(acc)
    for k, piece in enumerate(pieces):
        vectors[k * N_ZH : (k + 1) * N_ZH] = piece[...]

    def add(tile, rp, cp):
        acc[rp] += jnp.dot(tile, vectors[col_spot(place, cp)], preferred_element_type=F32)

    slot_loop(counts, rows, cols, blocks, add)


def products_of(kernel, scalars, blocks, pieces, n_out, out_blocks):
    edge, width = pieces[0].shape[1:]
    smem = pl.BlockSpec(memory_space=pltpu.SMEM)
    vmem = pl.BlockSpec(memory_space=pltpu.VMEM)
    n_in = len(pieces) * pieces[0].shape[0]
    return pl.pallas_call(
        kernel,
        out_shape=(jax.ShapeDtypeStruct((out_blocks, edge, width), F32),) * n_out,
        in_specs=[smem] * 4 + [vmem] * (1 + len(pieces)),
        out_specs=(vmem,) * n_out,
        scratch_shapes=[
            pltpu.VMEM((n_in, edge, width), jnp.bfloat16),
            pltpu.VMEM((n_out * out_blocks, edge, width), F32),
        ],
        cost_estimate=pl.CostEstimate(
            flops=2 * blocks.shape[0] * edge * edge * width,
            bytes_accessed=2 * blocks.size + 2 * n_in * edge * width + 4 * n_out * out_blocks * edge * width,
            transcendentals=0,
        ),
    )(*scalars, blocks, *pieces)


def spread(v):
    return jnp.broadcast_to(v, (SUB, LANES))


def eliminate(tiles, offset, done):
    below = lax.broadcasted_iota(jnp.int32, (SUB, LANES), 0) >= STEP
    for k in range(0, BLOCK, STEP):
        g, s = divmod(k, SUB)
        lane = offset + k
        head = tiles[g]
        rows = [spread(head[s + a : s + a + 1, :]) for a in range(STEP)]
        pivot = [[spread(head[s + a : s + a + 1, lane + b : lane + b + 1]) for b in range(a + 1)] for a in range(STEP)]
        rest = list(range(g if s == 0 else g + 1, len(tiles)))
        cols = {i: [spread(tiles[i][:, lane + a : lane + a + 1]) for a in range(STEP)] for i in rest}
        inverse = []
        for a in range(STEP):
            inverse.append(1.0 / pivot[a][a])
            for n in range(a + 1, STEP):
                ratio = pivot[n][a] * inverse[a]
                for b in range(a + 1, n + 1):
                    pivot[n][b] = pivot[n][b] - ratio * pivot[b][a]
                rows[n] = rows[n] - ratio * rows[a]
                for i in rest:
                    cols[i][n] = cols[i][n] - ratio * cols[i][a]
        for a in range(STEP):
            done[k + a : k + a + 1, :] = (rows[a] * lax.rsqrt(pivot[a][a]))[0:1, :]
        scaled = [rows[a] * inverse[a] for a in range(STEP)]
        for i in rest:
            take = (cols[i][0] * scaled[0] + cols[i][1] * scaled[1]) + (cols[i][2] * scaled[2] + cols[i][3] * scaled[3])
            if i == g:
                take = jnp.where(below, take, 0.0)
            tiles[i] = tiles[i] - take


def factor_kernel(place, piece0, piece1, piece2, piece3, products, basis, factor, work, done):
    edge, size = products.shape
    rows = size // (N_CORE * N_Y)
    my_core, my_y = place[0] & (N_CORE - 1), place[1] & (N_Y - 1)
    for k, piece in enumerate((piece0, piece1, piece2, piece3)):
        for side in range(N_CORE):
            at = (((my_core + side) & 1) * N_Y + ((my_y + k) & (N_Y - 1))) * rows
            work[pl.ds(pl.multiple_of(at, rows), rows), :size] = piece[side] * (1.0 / (N_ROW * N_COL * edge))
    work[:, size:] = products[...].T
    for p in range(size // BLOCK):
        top = p * BLOCK
        tile, offset = top // LANES * LANES, top % LANES
        lanes = lax.broadcasted_iota(jnp.int32, (SUB, LANES), 1)
        subs = lax.broadcasted_iota(jnp.int32, (SUB, LANES), 0)
        inside = (lanes >= offset) & (lanes < offset + BLOCK)
        tiles = []
        for i in range(BLOCK // SUB):
            unit = jnp.where(lanes == subs + (i * SUB + BLOCK - offset), 1.0, 0.0)
            part = work[top + i * SUB : top + (i + 1) * SUB, tile : tile + LANES]
            tiles.append(jnp.where(inside, part, unit))
        eliminate(tiles, offset, done)
        inside_all = lax.broadcasted_iota(jnp.int32, (BLOCK, LANES), 1) // BLOCK == offset // BLOCK
        inverse = jnp.where(inside_all, 0.0, done[...])
        panel = work[top : top + BLOCK, :]
        upper = jnp.dot(inverse, jnp.concatenate([panel, panel], 0), precision=lax.Precision.HIGHEST, preferred_element_type=F32)
        rows = lax.broadcasted_iota(jnp.int32, (BLOCK, size), 0) + top
        keep = lax.broadcasted_iota(jnp.int32, (BLOCK, size), 1) >= rows
        head = jnp.where(keep, upper[:, :size], 0.0)
        factor[top : top + BLOCK, :] = head
        work[top : top + BLOCK, size:] = upper[:, size:]
        if top + BLOCK < size:
            low = (top + BLOCK) // LANES * LANES
            full = jnp.concatenate([head, upper[:, size:]], 1)
            take = lax.dot_general(
                head[:, low:], full[:, low:], (((0,), (0,)), ((), ())), precision=lax.Precision.HIGHEST, preferred_element_type=F32
            )
            work[top + BLOCK :, low:] = work[top + BLOCK :, low:] - take[top + BLOCK - low :, :]
    basis[...] = work[:, size:].T


def factor_and_basis(place, pieces, products):
    edge, size = products.shape
    vmem = pl.BlockSpec(memory_space=pltpu.VMEM)
    return pl.pallas_call(
        factor_kernel,
        out_shape=(jax.ShapeDtypeStruct((edge, size), F32), jax.ShapeDtypeStruct((size, size), F32)),
        in_specs=[pl.BlockSpec(memory_space=pltpu.SMEM)] + [vmem] * 5,
        out_specs=(vmem, vmem),
        scratch_shapes=[pltpu.VMEM((size, size + edge), F32), pltpu.VMEM((BLOCK, LANES), F32)],
        name="factor",
    )(place, *pieces, products)


def gram_pieces(products, place):
    width = products.shape[1]
    half, piece = width // N_CORE, width // (N_CORE * N_Y)
    my_core, my_y = place[0] & (N_CORE - 1), place[1] & (N_Y - 1)
    local = jnp.dot(products.T, products, precision=lax.Precision.HIGHEST, preferred_element_type=F32)
    mine = lax.dynamic_slice_in_dim(local, my_core * half, half, 0)
    other = lax.dynamic_slice_in_dim(local, (1 - my_core) * half, half, 0)
    pair = mine + to_core(other)
    parts = [lax.dynamic_slice_in_dim(pair, ((my_y + k) & (N_Y - 1)) * piece, piece, 0) for k in range(N_Y)]
    got = ring_sum([parts[0]] + [to_y(parts[k], k) for k in range(1, N_Y)])
    got = ring_sum([got] + [to_x(got, k) for k in range(1, N_X)])
    got = got + to_zl(got)
    got = ring_sum(swap_z(copies(got, N_ZH)))
    both = jnp.stack([got, to_core(got)])
    return [both] + [to_y(both, -k) for k in range(1, N_Y)]


def body(blocks, block_rows, block_cols, counts, trials):
    place = jnp.stack([lax.axis_index("row"), lax.axis_index("col")]).astype(jnp.int32)
    scalars = (place, counts, block_rows, block_cols)
    first = jnp.stack([trials, to_zl(trials)])
    zs = swap_z(copies(trials, N_ZH))
    row_pieces = [first] + [to_y(first, -k) for k in range(1, N_Y)]
    col_pieces = [zs] + [to_x(zs, -k) for k in range(1, N_X)]
    col_keep, col_send = products_of(mirror_kernel, scalars, blocks[0], row_pieces, N_CORE, N_X * N_ZH)
    col_pieces = col_pieces + [to_core(v) for v in col_pieces]
    (row_out,) = products_of(direct_kernel, scalars, blocks[0], col_pieces, 1, N_COL)
    pair = col_keep + to_core(col_send)
    parts = [pair[k * N_ZH : (k + 1) * N_ZH] for k in range(N_X)]
    got = ring_sum([parts[0]] + [to_x(parts[k], k) for k in range(1, N_X)])
    row_sum = lax.all_to_all(row_out, "col", 0, 0, tiled=True).sum(0)
    col_sum = ring_sum(swap_z(got))
    products = row_sum + col_sum
    return factor_and_basis(place, gram_pieces(products, place), products)


def solution(mesh):
    return jax.shard_map(
        body,
        mesh=mesh,
        in_specs=(
            P("row", "col", None, None),
            P("row", "col"),
            P("row", "col"),
            P("row", "col"),
            P(("col", "row"), None),
        ),
        out_specs=(P(("col", "row"), None), P()),
        check_vma=False,
    )
```

```python
import jax
import jax.numpy as jnp
from jax import lax
from jax.experimental import pallas as pl
from jax.experimental.pallas import tpu as pltpu
from jax.sharding import PartitionSpec as P


N_ZH, N_X, N_CORE, N_ZL, N_Y = 4, 4, 2, 2, 4
N_ROW = N_ZH * N_X * N_CORE
N_COL = N_ZL * N_Y
F32 = jnp.float32
BLOCK, STEP, SUB, LANES = 64, 4, 8, 128


def row_at(z, x, c):
    return ((z % N_ZH) * N_X + x % N_X) * N_CORE + c


def col_at(zl, y):
    return zl * N_Y + y % N_Y


def row_pairs(move):
    return [(row_at(z, x, c), row_at(*move(z, x, c))) for z in range(N_ZH) for x in range(N_X) for c in range(N_CORE)]


def to_z(v, k):
    return lax.ppermute(v, "row", row_pairs(lambda z, x, c: (z + k, x, c)))


def to_x(v, k):
    return lax.ppermute(v, "row", row_pairs(lambda z, x, c: (z, x + k, c)))


def to_core(v):
    return lax.ppermute(v, "row", row_pairs(lambda z, x, c: (z, x, 1 - c)))


def to_y(v, k):
    return lax.ppermute(v, "col", [(col_at(zl, y), col_at(zl, y + k)) for zl in range(N_ZL) for y in range(N_Y)])


def to_zl(v):
    return lax.ppermute(v, "col", [(col_at(zl, y), col_at(1 - zl, y)) for zl in range(N_ZL) for y in range(N_Y)])


def ring_sum(parts):
    return (parts[0] + parts[2]) + (parts[1] + parts[3])


def slot_loop(counts, rows, cols, blocks, add):
    live = counts[0, 0]

    def visit(s):
        i, j = rows[0, s], cols[0, s]
        q = jnp.where(s < live, jnp.where(i == j, 0.5, 1.0), 0.0)
        tile = jnp.where(q > 0.0, blocks[s].astype(F32) * q, 0.0).astype(jnp.bfloat16)
        add(tile, i >> 5, j & (N_ROW - 1))

    def group(g, carry):
        for u in range(4):
            visit(g * 4 + u)
        return carry

    lax.fori_loop(0, (live + 3) // 4, group, 0)


def row_spot(place, rp):
    return ((rp - place[1]) & 3) * N_ZL + ((rp >> 2) ^ (place[1] >> 2))


def col_spot(place, cp):
    r = place[0]
    zk, xk, cx = ((cp >> 3) - (r >> 3)) & 3, ((cp >> 1) - (r >> 1)) & 3, (cp ^ r) & 1
    return cx * N_X * N_ZH, xk, zk


def mirror_kernel(place, counts, rows, cols, blocks, *refs):
    pieces, outs, vectors, acc = refs[:N_Y], refs[N_Y : N_Y + N_CORE], refs[-2], refs[-1]
    acc[...] = jnp.zeros_like(acc)
    for k, piece in enumerate(pieces):
        vectors[k * N_ZL : (k + 1) * N_ZL] = piece[...]

    def add(tile, rp, cp):
        base, xk, zk = col_spot(place, cp)
        acc[base + xk * N_ZH + zk] += lax.dot_general(
            tile, vectors[row_spot(place, rp)], (((0,), (0,)), ((), ())), preferred_element_type=F32
        )

    slot_loop(counts, rows, cols, blocks, add)
    for k, out in enumerate(outs):
        out[...] = acc[k * N_X * N_ZH : (k + 1) * N_X * N_ZH]


def direct_kernel(place, counts, rows, cols, blocks, *refs):
    n = N_CORE * N_ZH
    pieces, outs, vectors, acc = refs[:n], refs[n : n + N_Y], refs[-2], refs[-1]
    acc[...] = jnp.zeros_like(acc)
    for k, piece in enumerate(pieces):
        vectors[k * N_X : (k + 1) * N_X] = piece[...]

    def add(tile, rp, cp):
        base, xk, zk = col_spot(place, cp)
        acc[row_spot(place, rp)] += jnp.dot(tile, vectors[base + zk * N_X + xk], preferred_element_type=F32)

    slot_loop(counts, rows, cols, blocks, add)
    for k, out in enumerate(outs):
        out[...] = acc[k * N_ZL : (k + 1) * N_ZL]


def products_of(kernel, scalars, blocks, pieces, n_out, out_blocks):
    edge, width = pieces[0].shape[1:]
    smem = pl.BlockSpec(memory_space=pltpu.SMEM)
    vmem = pl.BlockSpec(memory_space=pltpu.VMEM)
    n_in = len(pieces) * pieces[0].shape[0]
    return pl.pallas_call(
        kernel,
        out_shape=(jax.ShapeDtypeStruct((out_blocks, edge, width), F32),) * n_out,
        in_specs=[smem] * 4 + [vmem] * (1 + len(pieces)),
        out_specs=(vmem,) * n_out,
        scratch_shapes=[
            pltpu.VMEM((n_in, edge, width), jnp.bfloat16),
            pltpu.VMEM((n_out * out_blocks, edge, width), F32),
        ],
        cost_estimate=pl.CostEstimate(
            flops=2 * blocks.shape[0] * edge * edge * width,
            bytes_accessed=2 * blocks.size + 2 * n_in * edge * width + 4 * n_out * out_blocks * edge * width,
            transcendentals=0,
        ),
    )(*scalars, blocks, *pieces)


def spread(v):
    return jnp.broadcast_to(v, (SUB, LANES))


def eliminate(tiles, offset, done):
    below = lax.broadcasted_iota(jnp.int32, (SUB, LANES), 0) >= STEP
    for k in range(0, BLOCK, STEP):
        g, s = divmod(k, SUB)
        lane = offset + k
        head = tiles[g]
        rows = [spread(head[s + a : s + a + 1, :]) for a in range(STEP)]
        pivot = [[spread(head[s + a : s + a + 1, lane + b : lane + b + 1]) for b in range(a + 1)] for a in range(STEP)]
        rest = list(range(g if s == 0 else g + 1, len(tiles)))
        cols = {i: [spread(tiles[i][:, lane + a : lane + a + 1]) for a in range(STEP)] for i in rest}
        inverse = []
        for a in range(STEP):
            inverse.append(1.0 / pivot[a][a])
            for n in range(a + 1, STEP):
                ratio = pivot[n][a] * inverse[a]
                for b in range(a + 1, n + 1):
                    pivot[n][b] = pivot[n][b] - ratio * pivot[b][a]
                rows[n] = rows[n] - ratio * rows[a]
                for i in rest:
                    cols[i][n] = cols[i][n] - ratio * cols[i][a]
        for a in range(STEP):
            done[k + a : k + a + 1, :] = (rows[a] * lax.rsqrt(pivot[a][a]))[0:1, :]
        scaled = [rows[a] * inverse[a] for a in range(STEP)]
        for i in rest:
            take = (cols[i][0] * scaled[0] + cols[i][1] * scaled[1]) + (cols[i][2] * scaled[2] + cols[i][3] * scaled[3])
            if i == g:
                take = jnp.where(below, take, 0.0)
            tiles[i] = tiles[i] - take


def factor_kernel(place, piece0, piece1, piece2, piece3, products, basis, factor, work, done):
    edge, size = products.shape
    rows = size // (N_CORE * N_Y)
    my_core, my_y = place[0] & (N_CORE - 1), place[1] & (N_Y - 1)
    for k, piece in enumerate((piece0, piece1, piece2, piece3)):
        for side in range(N_CORE):
            at = (((my_core + side) & 1) * N_Y + ((my_y + k) & (N_Y - 1))) * rows
            work[pl.ds(pl.multiple_of(at, rows), rows), :size] = piece[side] * (1.0 / (N_ROW * N_COL * edge))
    work[:, size:] = products[...].T
    for p in range(size // BLOCK):
        top = p * BLOCK
        tile, offset = top // LANES * LANES, top % LANES
        lanes = lax.broadcasted_iota(jnp.int32, (SUB, LANES), 1)
        subs = lax.broadcasted_iota(jnp.int32, (SUB, LANES), 0)
        inside = (lanes >= offset) & (lanes < offset + BLOCK)
        tiles = []
        for i in range(BLOCK // SUB):
            unit = jnp.where(lanes == subs + (i * SUB + BLOCK - offset), 1.0, 0.0)
            part = work[top + i * SUB : top + (i + 1) * SUB, tile : tile + LANES]
            tiles.append(jnp.where(inside, part, unit))
        eliminate(tiles, offset, done)
        inside_all = lax.broadcasted_iota(jnp.int32, (BLOCK, LANES), 1) // BLOCK == offset // BLOCK
        inverse = jnp.where(inside_all, 0.0, done[...])
        panel = work[top : top + BLOCK, :]
        upper = jnp.dot(inverse, jnp.concatenate([panel, panel], 0), precision=lax.Precision.HIGHEST, preferred_element_type=F32)
        rows = lax.broadcasted_iota(jnp.int32, (BLOCK, size), 0) + top
        keep = lax.broadcasted_iota(jnp.int32, (BLOCK, size), 1) >= rows
        head = jnp.where(keep, upper[:, :size], 0.0)
        factor[top : top + BLOCK, :] = head
        work[top : top + BLOCK, size:] = upper[:, size:]
        if top + BLOCK < size:
            low = (top + BLOCK) // LANES * LANES
            full = jnp.concatenate([head, upper[:, size:]], 1)
            take = lax.dot_general(
                head[:, low:], full[:, low:], (((0,), (0,)), ((), ())), precision=lax.Precision.HIGHEST, preferred_element_type=F32
            )
            work[top + BLOCK :, low:] = work[top + BLOCK :, low:] - take[top + BLOCK - low :, :]
    basis[...] = work[:, size:].T


def factor_and_basis(place, pieces, products):
    edge, size = products.shape
    vmem = pl.BlockSpec(memory_space=pltpu.VMEM)
    return pl.pallas_call(
        factor_kernel,
        out_shape=(jax.ShapeDtypeStruct((edge, size), F32), jax.ShapeDtypeStruct((size, size), F32)),
        in_specs=[pl.BlockSpec(memory_space=pltpu.SMEM)] + [vmem] * 5,
        out_specs=(vmem, vmem),
        scratch_shapes=[pltpu.VMEM((size, size + edge), F32), pltpu.VMEM((BLOCK, LANES), F32)],
        name="factor",
    )(place, *pieces, products)


def gram_pieces(products, place):
    width = products.shape[1]
    half, piece = width // N_CORE, width // (N_CORE * N_Y)
    my_core, my_y = place[0] & (N_CORE - 1), place[1] & (N_Y - 1)
    local = jnp.dot(products.T, products, precision=lax.Precision.HIGHEST, preferred_element_type=F32)
    mine = lax.dynamic_slice_in_dim(local, my_core * half, half, 0)
    other = lax.dynamic_slice_in_dim(local, (1 - my_core) * half, half, 0)
    pair = mine + to_core(other)
    parts = [lax.dynamic_slice_in_dim(pair, ((my_y + k) & (N_Y - 1)) * piece, piece, 0) for k in range(N_Y)]
    got = ring_sum([parts[0]] + [to_y(parts[k], k) for k in range(1, N_Y)])
    got = ring_sum([got] + [to_x(got, k) for k in range(1, N_X)])
    got = got + to_zl(got)
    got = ring_sum([got] + [to_z(got, k) for k in range(1, N_ZH)])
    both = jnp.stack([got, to_core(got)])
    return [both] + [to_y(both, -k) for k in range(1, N_Y)]


def body(blocks, block_rows, block_cols, counts, trials):
    place = jnp.stack([lax.axis_index("row"), lax.axis_index("col")]).astype(jnp.int32)
    scalars = (place, counts, block_rows, block_cols)
    first = jnp.stack([trials, to_zl(trials)])
    xs = jnp.stack([trials] + [to_x(trials, -k) for k in range(1, N_X)])
    row_pieces = [first] + [to_y(first, -k) for k in range(1, N_Y)]
    col_pieces = [xs] + [to_z(xs, -k) for k in range(1, N_ZH)]
    col_keep, col_send = products_of(mirror_kernel, scalars, blocks[0], row_pieces, N_CORE, N_X * N_ZH)
    col_pieces = col_pieces + [to_core(v) for v in col_pieces]
    row_outs = products_of(direct_kernel, scalars, blocks[0], col_pieces, N_Y, N_ZL)
    pair = col_keep + to_core(col_send)
    parts = [pair[k * N_ZH : (k + 1) * N_ZH] for k in range(N_X)]
    got = ring_sum([parts[0]] + [to_x(parts[k], k) for k in range(1, N_X)])
    rows = ring_sum([row_outs[0]] + [to_y(row_outs[k], k) for k in range(1, N_Y)])
    row_sum = rows[0] + to_zl(rows[1])
    col_sum = ring_sum([got[0]] + [to_z(got[k], k) for k in range(1, N_ZH)])
    products = row_sum + col_sum
    return factor_and_basis(place, gram_pieces(products, place), products)


def solution(mesh):
    return jax.shard_map(
        body,
        mesh=mesh,
        in_specs=(
            P("row", "col", None, None),
            P("row", "col"),
            P("row", "col"),
            P("row", "col"),
            P(("col", "row"), None),
        ),
        out_specs=(P(("col", "row"), None), P()),
        check_vma=False,
    )
```

```python
import jax
import jax.numpy as jnp
from jax import lax
from jax.experimental import pallas as pl
from jax.experimental.pallas import tpu as pltpu
from jax.sharding import PartitionSpec as P


N_ZH, N_X, N_CORE, N_ZL, N_Y = 4, 4, 2, 2, 4
N_ROW = N_ZH * N_X * N_CORE
N_COL = N_ZL * N_Y
F32 = jnp.float32
BLOCK, SUB, LANES = 64, 8, 128
STEP = SUB


def row_at(z, x, c):
    return ((z % N_ZH) * N_X + x % N_X) * N_CORE + c


def col_at(zl, y):
    return zl * N_Y + y % N_Y


def row_pairs(move):
    return [(row_at(z, x, c), row_at(*move(z, x, c))) for z in range(N_ZH) for x in range(N_X) for c in range(N_CORE)]


def to_z(v, k):
    return lax.ppermute(v, "row", row_pairs(lambda z, x, c: (z + k, x, c)))


def to_x(v, k):
    return lax.ppermute(v, "row", row_pairs(lambda z, x, c: (z, x + k, c)))


def to_core(v):
    return lax.ppermute(v, "row", row_pairs(lambda z, x, c: (z, x, 1 - c)))


def to_y(v, k):
    return lax.ppermute(v, "col", [(col_at(zl, y), col_at(zl, y + k)) for zl in range(N_ZL) for y in range(N_Y)])


def to_zl(v):
    return lax.ppermute(v, "col", [(col_at(zl, y), col_at(1 - zl, y)) for zl in range(N_ZL) for y in range(N_Y)])


def ring_sum(parts):
    return (parts[0] + parts[2]) + (parts[1] + parts[3])


def clear(acc):
    def one(n, carry):
        acc[n] = jnp.zeros(acc.shape[1:], acc.dtype)
        return carry

    lax.fori_loop(0, acc.shape[0], one, 0)


def hand_out(acc, outs):
    for k, out in enumerate(outs):
        size = out.shape[0]

        def one(n, carry):
            out[n] = acc[k * size + n]
            return carry

        lax.fori_loop(0, size, one, 0)


def slot_loop(counts, rows, cols, blocks, add):
    live = counts[0, 0]

    def visit(s):
        i, j = rows[0, s], cols[0, s]
        q = jnp.where(s < live, jnp.where(i == j, 0.5, 1.0), 0.0)
        tile = jnp.where(q > 0.0, blocks[s].astype(F32) * q, 0.0).astype(jnp.bfloat16)
        add(tile, i >> 5, j & (N_ROW - 1))

    def group(g, carry):
        for u in range(4):
            visit(g * 4 + u)
        return carry

    lax.fori_loop(0, (live + 3) // 4, group, 0)


def row_spot(place, rp):
    return ((rp - place[1]) & 3) * N_ZL + ((rp >> 2) ^ (place[1] >> 2))


def col_spot(place, cp):
    r = place[0]
    zk, xk, cx = ((cp >> 3) - (r >> 3)) & 3, ((cp >> 1) - (r >> 1)) & 3, (cp ^ r) & 1
    return cx * N_X * N_ZH, xk, zk


def mirror_kernel(place, counts, rows, cols, blocks, *refs):
    pieces, outs, vectors, acc = refs[:N_Y], refs[N_Y:-2], refs[-2], refs[-1]
    clear(acc)
    for k, piece in enumerate(pieces):
        vectors[k * N_ZL : (k + 1) * N_ZL] = piece[...]

    def add(tile, rp, cp):
        base, xk, zk = col_spot(place, cp)
        acc[base + xk * N_ZH + zk] += lax.dot_general(
            tile, vectors[row_spot(place, rp)], (((0,), (0,)), ((), ())), preferred_element_type=F32
        )

    slot_loop(counts, rows, cols, blocks, add)
    hand_out(acc, outs)


def direct_kernel(place, counts, rows, cols, blocks, *refs):
    n = N_CORE * N_ZH
    pieces, outs, vectors, acc = refs[:n], refs[n : n + N_Y], refs[-2], refs[-1]
    clear(acc)
    for k, piece in enumerate(pieces):
        vectors[k * N_X : (k + 1) * N_X] = piece[...]

    def add(tile, rp, cp):
        base, xk, zk = col_spot(place, cp)
        acc[row_spot(place, rp)] += jnp.dot(tile, vectors[base + zk * N_X + xk], preferred_element_type=F32)

    slot_loop(counts, rows, cols, blocks, add)
    hand_out(acc, outs)


def products_of(kernel, scalars, blocks, pieces, n_out, out_blocks):
    edge, width = pieces[0].shape[1:]
    smem = pl.BlockSpec(memory_space=pltpu.SMEM)
    vmem = pl.BlockSpec(memory_space=pltpu.VMEM)
    n_in = len(pieces) * pieces[0].shape[0]
    return pl.pallas_call(
        kernel,
        out_shape=(jax.ShapeDtypeStruct((out_blocks, edge, width), F32),) * n_out,
        in_specs=[smem] * 4 + [vmem] * (1 + len(pieces)),
        out_specs=(vmem,) * n_out,
        scratch_shapes=[
            pltpu.VMEM((n_in, edge, width), jnp.bfloat16),
            pltpu.VMEM((n_out * out_blocks, edge, width), F32),
        ],
        cost_estimate=pl.CostEstimate(
            flops=2 * blocks.shape[0] * edge * edge * width,
            bytes_accessed=2 * blocks.size + 2 * n_in * edge * width + 4 * n_out * out_blocks * edge * width,
            transcendentals=0,
        ),
        compiler_params=pltpu.CompilerParams(vmem_limit_bytes=16 << 20),
    )(*scalars, blocks, *pieces)


def spread(v):
    return jnp.broadcast_to(v, (SUB, LANES))


def eliminate(tiles, done):
    for g in range(BLOCK // STEP):
        k = lane = g * STEP
        head = tiles[g]
        rows = [spread(head[a : a + 1, :]) for a in range(STEP)]
        pivot = [[spread(head[a : a + 1, lane + b : lane + b + 1]) for b in range(a + 1)] for a in range(STEP)]
        rest = list(range(g + 1, len(tiles)))
        cols = {i: [spread(tiles[i][:, lane + a : lane + a + 1]) for a in range(STEP)] for i in rest}
        inverse = []
        for a in range(STEP):
            inverse.append(1.0 / pivot[a][a])
            for n in range(a + 1, STEP):
                ratio = pivot[n][a] * inverse[a]
                for b in range(a + 1, n + 1):
                    pivot[n][b] = pivot[n][b] - ratio * pivot[b][a]
                rows[n] = rows[n] - ratio * rows[a]
                for i in rest:
                    cols[i][n] = cols[i][n] - ratio * cols[i][a]
        for a in range(STEP):
            done[k + a : k + a + 1, :] = (rows[a] * lax.rsqrt(pivot[a][a]))[0:1, :]
        scaled = [rows[a] * inverse[a] for a in range(STEP)]
        for i in rest:
            terms = [cols[i][a] * scaled[a] for a in range(STEP)]
            while len(terms) > 1:
                terms = [terms[m] + terms[m + 1] for m in range(0, len(terms), 2)]
            tiles[i] = tiles[i] - terms[0]


def set_stage(work, stage, top):
    tile, offset = top // LANES * LANES, top % LANES
    part = work[top : top + BLOCK, tile : tile + LANES]
    if offset:
        part = pltpu.roll(part, BLOCK, 1)
    lanes = lax.broadcasted_iota(jnp.int32, (BLOCK, LANES), 1)
    unit = jnp.where(lanes == lax.broadcasted_iota(jnp.int32, (BLOCK, LANES), 0) + BLOCK, 1.0, 0.0)
    stage[...] = jnp.where(lanes < BLOCK, part, unit)


def apply_block(work, stage, done, factor, top):
    size = factor.shape[1]
    lanes = lax.broadcasted_iota(jnp.int32, (BLOCK, LANES), 1)
    inverse = jnp.where(lanes < BLOCK, 0.0, done[...])
    panel = work[top : top + BLOCK, :]
    upper = jnp.dot(
        inverse, jnp.concatenate([panel, panel], 0), precision=lax.Precision.HIGHEST, preferred_element_type=F32
    )
    rows = lax.broadcasted_iota(jnp.int32, (BLOCK, size), 0) + top
    keep = lax.broadcasted_iota(jnp.int32, (BLOCK, size), 1) >= rows
    head = jnp.where(keep, upper[:, :size], 0.0)
    factor[top : top + BLOCK, :] = head
    work[top : top + BLOCK, size:] = upper[:, size:]
    if top + BLOCK < size:
        low = (top + BLOCK) // LANES * LANES
        full = jnp.concatenate([head, upper[:, size:]], 1)
        take = lax.dot_general(
            head[:, low:],
            full[:, low:],
            (((0,), (0,)), ((), ())),
            precision=lax.Precision.HIGHEST,
            preferred_element_type=F32,
        )
        work[top + BLOCK :, low:] = work[top + BLOCK :, low:] - take[top + BLOCK - low :, :]
        set_stage(work, stage, top + BLOCK)


def factor_kernel(place, piece0, piece1, piece2, piece3, products, basis, factor, work, stage, done):
    edge, size = products.shape
    rows = size // (N_CORE * N_Y)
    my_core, my_y = place[0] & (N_CORE - 1), place[1] & (N_Y - 1)
    for k, piece in enumerate((piece0, piece1, piece2, piece3)):
        for side in range(N_CORE):
            at = (((my_core + side) & 1) * N_Y + ((my_y + k) & (N_Y - 1))) * rows
            work[pl.ds(pl.multiple_of(at, rows), rows), :size] = piece[side] * (1.0 / (N_ROW * N_COL * edge))
    work[:, size:] = products[...].T
    set_stage(work, stage, 0)

    def block(p, carry):
        eliminate([stage[i * SUB : (i + 1) * SUB, :] for i in range(BLOCK // SUB)], done)
        for q in range(size // BLOCK):
            pl.when(p == q)(lambda q=q: apply_block(work, stage, done, factor, q * BLOCK))
        return carry

    lax.fori_loop(0, size // BLOCK, block, 0)
    basis[...] = work[:, size:].T


def factor_and_basis(place, pieces, products):
    edge, size = products.shape
    vmem = pl.BlockSpec(memory_space=pltpu.VMEM)
    return pl.pallas_call(
        factor_kernel,
        out_shape=(jax.ShapeDtypeStruct((edge, size), F32), jax.ShapeDtypeStruct((size, size), F32)),
        in_specs=[pl.BlockSpec(memory_space=pltpu.SMEM)] + [vmem] * 5,
        out_specs=(vmem, vmem),
        scratch_shapes=[pltpu.VMEM((size, size + edge), F32)] + [pltpu.VMEM((BLOCK, LANES), F32)] * 2,
        compiler_params=pltpu.CompilerParams(vmem_limit_bytes=8 << 20),
        name="factor",
    )(place, *pieces, products)


def gram_pieces(products, place):
    width = products.shape[1]
    half, piece = width // N_CORE, width // (N_CORE * N_Y)
    my_core, my_y = place[0] & (N_CORE - 1), place[1] & (N_Y - 1)
    local = jnp.dot(products.T, products, precision=lax.Precision.HIGHEST, preferred_element_type=F32)
    mine = lax.dynamic_slice_in_dim(local, my_core * half, half, 0)
    other = lax.dynamic_slice_in_dim(local, (1 - my_core) * half, half, 0)
    pair = mine + to_core(other)
    parts = [lax.dynamic_slice_in_dim(pair, ((my_y + k) & (N_Y - 1)) * piece, piece, 0) for k in range(N_Y)]
    got = ring_sum([parts[0]] + [to_y(parts[k], k) for k in range(1, N_Y)])
    got = ring_sum([got] + [to_x(got, k) for k in range(1, N_X)])
    got = got + to_zl(got)
    got = ring_sum([got] + [to_z(got, k) for k in range(1, N_ZH)])
    both = jnp.stack([got, to_core(got)])
    return [both] + [to_y(both, -k) for k in range(1, N_Y)]


def body(blocks, block_rows, block_cols, counts, trials):
    place = jnp.stack([lax.axis_index("row"), lax.axis_index("col")]).astype(jnp.int32)
    scalars = (place, counts, block_rows, block_cols)
    first = jnp.stack([trials, to_zl(trials)])
    xs = jnp.stack([trials] + [to_x(trials, -k) for k in range(1, N_X)])
    row_pieces = [first] + [to_y(first, -k) for k in range(1, N_Y)]
    col_pieces = [xs] + [to_z(xs, -k) for k in range(1, N_ZH)]
    outs = products_of(mirror_kernel, scalars, blocks[0], row_pieces, N_CORE * N_X, N_ZH)
    keep, send = outs[:N_X], outs[N_X:]
    col_pieces = col_pieces + [to_core(v) for v in col_pieces]
    row_outs = products_of(direct_kernel, scalars, blocks[0], col_pieces, N_Y, N_ZL)
    theirs = {k: to_core(send[k]) for k in (1, 3, 2, 0)}
    sent = {k: to_x(keep[k] + theirs[k], k) for k in (1, 3, 2)}
    got = ring_sum([keep[0] + theirs[0]] + [sent[k] for k in range(1, N_X)])
    rows = ring_sum([row_outs[0]] + [to_y(row_outs[k], k) for k in range(1, N_Y)])
    row_sum = rows[0] + to_zl(rows[1])
    col_sum = ring_sum([got[0]] + [to_z(got[k], k) for k in range(1, N_ZH)])
    products = row_sum + col_sum
    return factor_and_basis(place, gram_pieces(products, place), products)


def solution(mesh):
    return jax.shard_map(
        body,
        mesh=mesh,
        in_specs=(
            P("row", "col", None, None),
            P("row", "col"),
            P("row", "col"),
            P("row", "col"),
            P(("col", "row"), None),
        ),
        out_specs=(P(("col", "row"), None), P()),
        check_vma=False,
    )
```

```python
import jax
import jax.numpy as jnp
from jax import lax
from jax.experimental import pallas as pl
from jax.experimental.pallas import tpu as pltpu
from jax.sharding import PartitionSpec as P


N_ZH, N_X, N_CORE, N_ZL, N_Y = 4, 4, 2, 2, 4
N_ROW = N_ZH * N_X * N_CORE
N_COL = N_ZL * N_Y
F32 = jnp.float32
BLOCK, SUB, LANES = 64, 8, 128
STEP = SUB
CHUNK = 8


def row_at(z, x, c):
    return ((z % N_ZH) * N_X + x % N_X) * N_CORE + c


def col_at(zl, y):
    return zl * N_Y + y % N_Y


def row_pairs(move):
    return [(row_at(z, x, c), row_at(*move(z, x, c))) for z in range(N_ZH) for x in range(N_X) for c in range(N_CORE)]


def to_z(v, k):
    return lax.ppermute(v, "row", row_pairs(lambda z, x, c: (z + k, x, c)))


def to_x(v, k):
    return lax.ppermute(v, "row", row_pairs(lambda z, x, c: (z, x + k, c)))


def to_core(v):
    return lax.ppermute(v, "row", row_pairs(lambda z, x, c: (z, x, 1 - c)))


def to_y(v, k):
    return lax.ppermute(v, "col", [(col_at(zl, y), col_at(zl, y + k)) for zl in range(N_ZL) for y in range(N_Y)])


def to_col(v, k, flip):
    return lax.ppermute(
        v, "col", [(col_at(zl, y), col_at(zl ^ flip, y + k)) for zl in range(N_ZL) for y in range(N_Y)]
    )


def to_zl(v):
    return to_col(v, 0, 1)


def ring_sum(parts):
    return (parts[0] + parts[2]) + (parts[1] + parts[3])


def clear(acc):
    def one(n, carry):
        acc[n] = jnp.zeros(acc.shape[1:], acc.dtype)
        return carry

    lax.fori_loop(0, acc.shape[0], one, 0)


def hand_out(acc, outs):
    for k, out in enumerate(outs):
        size = out.shape[0]

        def one(n, carry):
            out[n] = acc[k * size + n]
            return carry

        lax.fori_loop(0, size, one, 0)


def slot_loop(table, blocks, tiles, sems, prepare, add):
    live = table[2, 0]
    chunks = (live + CHUNK - 1) // CHUNK

    def fetch(n):
        return pltpu.make_async_copy(
            blocks.at[pl.ds(n * CHUNK, CHUNK)], tiles.at[pl.ds(n * CHUNK, CHUNK)], sems.at[n]
        )

    def start(n, carry):
        fetch(n).start()
        return carry

    def visit(s):
        i, j = table[0, s], table[1, s]
        q = jnp.where(s < live, jnp.where(i == j, 0.5, 1.0), 0.0)
        tile = jnp.where(q > 0.0, tiles[s].astype(F32) * q, 0.0).astype(jnp.bfloat16)
        add(tile, i >> 5, j & (N_ROW - 1))

    def chunk(n, carry):
        fetch(n).wait()

        def group(g, inner):
            for u in range(4):
                visit(n * CHUNK + g * 4 + u)
            return inner

        return lax.fori_loop(0, CHUNK // 4, group, carry)

    lax.fori_loop(0, chunks, start, 0)
    prepare()
    lax.fori_loop(0, chunks, chunk, 0)


def row_spot(table, rp):
    c = table[3, 1]
    return ((rp - c) & 3) * N_ZL + ((rp ^ c) >> 2)


def col_spot(table, cp):
    r = table[3, 0]
    zk, xk, cx = ((cp >> 3) - (r >> 3)) & 3, ((cp >> 1) - (r >> 1)) & 3, (cp ^ r) & 1
    return cx * N_X * N_ZH, xk, zk


def mirror_kernel(table, blocks, *refs):
    pieces, outs, (vectors, acc, tiles, sems) = refs[:N_Y], refs[N_Y:-4], refs[-4:]

    def prepare():
        clear(acc)
        for k, piece in enumerate(pieces):
            vectors[k * N_ZL : (k + 1) * N_ZL] = piece[...]

    def add(tile, rp, cp):
        base, xk, zk = col_spot(table, cp)
        acc[base + xk * N_ZH + zk] += lax.dot_general(
            tile, vectors[row_spot(table, rp)], (((0,), (0,)), ((), ())), preferred_element_type=F32
        )

    slot_loop(table, blocks, tiles, sems, prepare, add)
    hand_out(acc, outs)


def direct_kernel(table, blocks, *refs):
    n = N_CORE * N_ZH
    pieces, outs, (vectors, acc, tiles, sems) = refs[:n], refs[n:-4], refs[-4:]

    def prepare():
        clear(acc)
        for k, piece in enumerate(pieces):
            vectors[k * N_X : (k + 1) * N_X] = piece[...]

    def add(tile, rp, cp):
        base, xk, zk = col_spot(table, cp)
        acc[row_spot(table, rp)] += jnp.dot(tile, vectors[base + zk * N_X + xk], preferred_element_type=F32)

    slot_loop(table, blocks, tiles, sems, prepare, add)
    hand_out(acc, outs)


def products_of(kernel, table, blocks, pieces, n_out, out_blocks):
    edge, width = pieces[0].shape[1:]
    vmem = pl.BlockSpec(memory_space=pltpu.VMEM)
    n_in = len(pieces) * pieces[0].shape[0]
    return pl.pallas_call(
        kernel,
        out_shape=(jax.ShapeDtypeStruct((out_blocks, edge, width), F32),) * n_out,
        in_specs=[pl.BlockSpec(memory_space=pltpu.SMEM), pl.BlockSpec(memory_space=pltpu.HBM)] + [vmem] * len(pieces),
        out_specs=(vmem,) * n_out,
        scratch_shapes=[
            pltpu.VMEM((n_in, edge, width), jnp.bfloat16),
            pltpu.VMEM((n_out * out_blocks, edge, width), F32),
            pltpu.VMEM(blocks.shape, blocks.dtype),
            pltpu.SemaphoreType.DMA((blocks.shape[0] // CHUNK,)),
        ],
        cost_estimate=pl.CostEstimate(
            flops=2 * blocks.shape[0] * edge * edge * width,
            bytes_accessed=2 * blocks.size + 2 * n_in * edge * width + 4 * n_out * out_blocks * edge * width,
            transcendentals=0,
        ),
        compiler_params=pltpu.CompilerParams(vmem_limit_bytes=16 << 20),
    )(table, pltpu.with_memory_space_constraint(blocks, pltpu.HBM), *pieces)


def spread(v):
    return jnp.broadcast_to(v, (SUB, LANES))


def eliminate(tiles, done):
    for g in range(BLOCK // STEP):
        k = lane = g * STEP
        head = tiles[g]
        rows = [spread(head[a : a + 1, :]) for a in range(STEP)]
        pivot = [[spread(head[a : a + 1, lane + b : lane + b + 1]) for b in range(a + 1)] for a in range(STEP)]
        rest = list(range(g + 1, len(tiles)))
        cols = {i: [spread(tiles[i][:, lane + a : lane + a + 1]) for a in range(STEP)] for i in rest}
        inverse = []
        for a in range(STEP):
            inverse.append(1.0 / pivot[a][a])
            for n in range(a + 1, STEP):
                ratio = pivot[n][a] * inverse[a]
                for b in range(a + 1, n + 1):
                    pivot[n][b] = pivot[n][b] - ratio * pivot[b][a]
                rows[n] = rows[n] - ratio * rows[a]
                for i in rest:
                    cols[i][n] = cols[i][n] - ratio * cols[i][a]
        for a in range(STEP):
            done[k + a : k + a + 1, :] = (rows[a] * lax.rsqrt(pivot[a][a]))[0:1, :]
        scaled = [rows[a] * inverse[a] for a in range(STEP)]
        for i in rest:
            terms = [cols[i][a] * scaled[a] for a in range(STEP)]
            while len(terms) > 1:
                terms = [terms[m] + terms[m + 1] for m in range(0, len(terms), 2)]
            tiles[i] = tiles[i] - terms[0]


def set_stage(work, stage, top):
    tile, offset = top // LANES * LANES, top % LANES
    part = work[top : top + BLOCK, tile : tile + LANES]
    if offset:
        part = pltpu.roll(part, BLOCK, 1)
    lanes = lax.broadcasted_iota(jnp.int32, (BLOCK, LANES), 1)
    unit = jnp.where(lanes == lax.broadcasted_iota(jnp.int32, (BLOCK, LANES), 0) + BLOCK, 1.0, 0.0)
    stage[...] = jnp.where(lanes < BLOCK, part, unit)


def apply_block(work, stage, done, factor, top):
    size = factor.shape[1]
    lanes = lax.broadcasted_iota(jnp.int32, (BLOCK, LANES), 1)
    inverse = jnp.where(lanes < BLOCK, 0.0, done[...])
    panel = work[top : top + BLOCK, :]
    upper = jnp.dot(
        inverse, jnp.concatenate([panel, panel], 0), precision=lax.Precision.HIGHEST, preferred_element_type=F32
    )
    rows = lax.broadcasted_iota(jnp.int32, (BLOCK, size), 0) + top
    keep = lax.broadcasted_iota(jnp.int32, (BLOCK, size), 1) >= rows
    head = jnp.where(keep, upper[:, :size], 0.0)
    factor[top : top + BLOCK, :] = head
    work[top : top + BLOCK, size:] = upper[:, size:]
    if top + BLOCK < size:
        low = (top + BLOCK) // LANES * LANES
        full = jnp.concatenate([head, upper[:, size:]], 1)
        take = lax.dot_general(
            head[:, low:],
            full[:, low:],
            (((0,), (0,)), ((), ())),
            precision=lax.Precision.HIGHEST,
            preferred_element_type=F32,
        )
        work[top + BLOCK :, low:] = work[top + BLOCK :, low:] - take[top + BLOCK - low :, :]
        set_stage(work, stage, top + BLOCK)


def factor_kernel(table, piece0, piece1, piece2, piece3, products, basis, factor, work, stage, done):
    edge, size = products.shape
    rows = size // (N_CORE * N_Y)
    my_core, my_y = table[3, 0] & (N_CORE - 1), table[3, 1] & (N_Y - 1)
    for k, piece in enumerate((piece0, piece1, piece2, piece3)):
        for side in range(N_CORE):
            at = (((my_core + side) & 1) * N_Y + ((my_y + k) & (N_Y - 1))) * rows
            work[pl.ds(pl.multiple_of(at, rows), rows), :size] = piece[side] * (1.0 / (N_ROW * N_COL * edge))
    work[:, size:] = products[...].T
    set_stage(work, stage, 0)

    def block(p, carry):
        eliminate([stage[i * SUB : (i + 1) * SUB, :] for i in range(BLOCK // SUB)], done)
        for q in range(size // BLOCK):
            pl.when(p == q)(lambda q=q: apply_block(work, stage, done, factor, q * BLOCK))
        return carry

    lax.fori_loop(0, size // BLOCK, block, 0)
    basis[...] = work[:, size:].T


def factor_and_basis(table, pieces, products):
    edge, size = products.shape
    vmem = pl.BlockSpec(memory_space=pltpu.VMEM)
    return pl.pallas_call(
        factor_kernel,
        out_shape=(jax.ShapeDtypeStruct((edge, size), F32), jax.ShapeDtypeStruct((size, size), F32)),
        in_specs=[pl.BlockSpec(memory_space=pltpu.SMEM)] + [vmem] * 5,
        out_specs=(vmem, vmem),
        scratch_shapes=[pltpu.VMEM((size, size + edge), F32)] + [pltpu.VMEM((BLOCK, LANES), F32)] * 2,
        compiler_params=pltpu.CompilerParams(vmem_limit_bytes=8 << 20),
        name="factor",
    )(table, *pieces, products)


def gram_pieces(products, r, c):
    width = products.shape[1]
    half, piece = width // N_CORE, width // (N_CORE * N_Y)
    my_core, my_y = r & (N_CORE - 1), c & (N_Y - 1)
    local = jnp.dot(products.T, products, precision=lax.Precision.HIGHEST, preferred_element_type=F32)
    mine = lax.dynamic_slice_in_dim(local, my_core * half, half, 0)
    other = lax.dynamic_slice_in_dim(local, (1 - my_core) * half, half, 0)
    pair = mine + to_core(other)
    parts = [lax.dynamic_slice_in_dim(pair, ((my_y + k) & (N_Y - 1)) * piece, piece, 0) for k in range(N_Y)]
    got = ring_sum([parts[0]] + [to_y(parts[k], k) for k in range(1, N_Y)])
    got = ring_sum([got] + [to_x(got, k) for k in range(1, N_X)])
    got = got + to_zl(got)
    got = ring_sum([got] + [to_z(got, k) for k in range(1, N_ZH)])
    both = jnp.stack([got, to_core(got)])
    return [both] + [to_y(both, -k) for k in range(1, N_Y)]


def body(blocks, block_rows, block_cols, counts, trials):
    r, c = lax.axis_index("row").astype(jnp.int32), lax.axis_index("col").astype(jnp.int32)
    slots = block_rows.shape[1]
    at = lax.broadcasted_iota(jnp.int32, (1, slots), 1)
    table = jnp.concatenate(
        [block_rows, block_cols, jnp.broadcast_to(counts, (1, slots)), jnp.where(at == 0, r, c)], 0
    )
    first = jnp.stack([trials, to_zl(trials)])
    xs = jnp.stack([trials] + [to_x(trials, -k) for k in range(1, N_X)])
    row_pieces = [first] + [to_y(first, -k) for k in range(1, N_Y)]
    col_pieces = [xs] + [to_z(xs, -k) for k in range(1, N_ZH)]
    outs = products_of(mirror_kernel, table, blocks[0], row_pieces, N_CORE * N_X, N_ZH)
    keep, send = outs[:N_X], outs[N_X:]
    col_pieces = col_pieces + [to_core(v) for v in col_pieces]
    row_outs = products_of(direct_kernel, table, blocks[0], col_pieces, N_COL, 1)
    theirs = {k: to_core(send[k]) for k in (1, 3, 2, 0)}
    sent = {k: to_x(keep[k] + theirs[k], k) for k in (1, 3, 2)}
    got = ring_sum([keep[0] + theirs[0]] + [sent[k] for k in range(1, N_X)])
    got_rows = [row_outs[0]]
    for n in range(1, N_COL):
        got_rows.append(to_col(row_outs[n], n // N_ZL, n % N_ZL))
    row_sum = (ring_sum(got_rows[:4]) + ring_sum(got_rows[4:]))[0]
    col_sum = ring_sum([got[0]] + [to_z(got[k], k) for k in range(1, N_ZH)])
    products = row_sum + col_sum
    return factor_and_basis(table, gram_pieces(products, r, c), products)


def solution(mesh):
    return jax.shard_map(
        body,
        mesh=mesh,
        in_specs=(
            P("row", "col", None, None),
            P("row", "col"),
            P("row", "col"),
            P("row", "col"),
            P(("col", "row"), None),
        ),
        out_specs=(P(("col", "row"), None), P()),
        check_vma=False,
    )
```

```python
import jax
import jax.numpy as jnp
from jax import lax
from jax.experimental import pallas as pl
from jax.experimental.pallas import tpu as pltpu
from jax.sharding import PartitionSpec as P


N_ZH, N_X, N_CORE, N_ZL, N_Y = 4, 4, 2, 2, 4
N_ROW = N_ZH * N_X * N_CORE
N_COL = N_ZL * N_Y
F32 = jnp.float32
BLOCK, SUB, LANES = 64, 8, 128
STEP = SUB
CHUNK = 8


def row_at(z, x, c):
    return ((z % N_ZH) * N_X + x % N_X) * N_CORE + c


def col_at(zl, y):
    return zl * N_Y + y % N_Y


def row_pairs(move):
    return [(row_at(z, x, c), row_at(*move(z, x, c))) for z in range(N_ZH) for x in range(N_X) for c in range(N_CORE)]


def to_z(v, k):
    return lax.ppermute(v, "row", row_pairs(lambda z, x, c: (z + k, x, c)))


def to_x(v, k):
    return lax.ppermute(v, "row", row_pairs(lambda z, x, c: (z, x + k, c)))


def to_core(v):
    return lax.ppermute(v, "row", row_pairs(lambda z, x, c: (z, x, 1 - c)))


def to_y(v, k):
    return lax.ppermute(v, "col", [(col_at(zl, y), col_at(zl, y + k)) for zl in range(N_ZL) for y in range(N_Y)])


def to_zl(v):
    return lax.ppermute(v, "col", [(col_at(zl, y), col_at(1 - zl, y)) for zl in range(N_ZL) for y in range(N_Y)])


def ring_sum(parts):
    return (parts[0] + parts[2]) + (parts[1] + parts[3])


def clear(acc):
    def one(n, carry):
        acc[n] = jnp.zeros(acc.shape[1:], acc.dtype)
        return carry

    lax.fori_loop(0, acc.shape[0], one, 0)


def hand_out(acc, outs):
    for k, out in enumerate(outs):
        size = out.shape[0]

        def one(n, carry):
            out[n] = acc[k * size + n]
            return carry

        lax.fori_loop(0, size, one, 0)


def slot_loop(table, blocks, tiles, sems, prepare, add):
    live = table[2, 0]
    chunks = (live + CHUNK - 1) // CHUNK

    def fetch(n):
        return pltpu.make_async_copy(
            blocks.at[pl.ds(n * CHUNK, CHUNK)], tiles.at[pl.ds(n * CHUNK, CHUNK)], sems.at[n]
        )

    def start(n, carry):
        fetch(n).start()
        return carry

    def visit(s):
        i, j = table[0, s], table[1, s]
        q = jnp.where(s < live, jnp.where(i == j, 0.5, 1.0), 0.0)
        tile = jnp.where(q > 0.0, tiles[s].astype(F32) * q, 0.0).astype(jnp.bfloat16)
        add(tile, i >> 5, j & (N_ROW - 1))

    def chunk(n, carry):
        fetch(n).wait()

        def group(g, inner):
            for u in range(4):
                visit(n * CHUNK + g * 4 + u)
            return inner

        return lax.fori_loop(0, CHUNK // 4, group, carry)

    lax.fori_loop(0, chunks, start, 0)
    prepare()
    lax.fori_loop(0, chunks, chunk, 0)


def row_spot(table, rp):
    c = table[3, 1]
    return ((rp - c) & 3) * N_ZL + ((rp ^ c) >> 2)


def col_spot(table, cp):
    r = table[3, 0]
    zk, xk, cx = ((cp >> 3) - (r >> 3)) & 3, ((cp >> 1) - (r >> 1)) & 3, (cp ^ r) & 1
    return cx * N_X * N_ZH + xk * N_ZH + zk


def mirror_kernel(table, blocks, *refs):
    pieces, outs, (vectors, acc, tiles, sems) = refs[:N_Y], refs[N_Y:-4], refs[-4:]

    def prepare():
        clear(acc)
        for k, piece in enumerate(pieces):
            vectors[k * N_ZL : (k + 1) * N_ZL] = piece[...]

    def add(tile, rp, cp):
        acc[col_spot(table, cp)] += lax.dot_general(
            tile, vectors[row_spot(table, rp)], (((0,), (0,)), ((), ())), preferred_element_type=F32
        )

    slot_loop(table, blocks, tiles, sems, prepare, add)
    hand_out(acc, outs)


def direct_kernel(table, blocks, *refs):
    n = N_CORE * N_X
    pieces, outs, (vectors, acc, tiles, sems) = refs[:n], refs[n:-4], refs[-4:]

    def prepare():
        clear(acc)
        for k, piece in enumerate(pieces):
            vectors[k * N_ZH : (k + 1) * N_ZH] = piece[...]

    def add(tile, rp, cp):
        acc[row_spot(table, rp)] += jnp.dot(tile, vectors[col_spot(table, cp)], preferred_element_type=F32)

    slot_loop(table, blocks, tiles, sems, prepare, add)
    hand_out(acc, outs)


def products_of(kernel, table, blocks, pieces, n_out, out_blocks):
    edge, width = pieces[0].shape[1:]
    vmem = pl.BlockSpec(memory_space=pltpu.VMEM)
    n_in = len(pieces) * pieces[0].shape[0]
    return pl.pallas_call(
        kernel,
        out_shape=(jax.ShapeDtypeStruct((out_blocks, edge, width), F32),) * n_out,
        in_specs=[pl.BlockSpec(memory_space=pltpu.SMEM), pl.BlockSpec(memory_space=pltpu.HBM)] + [vmem] * len(pieces),
        out_specs=(vmem,) * n_out,
        scratch_shapes=[
            pltpu.VMEM((n_in, edge, width), jnp.bfloat16),
            pltpu.VMEM((n_out * out_blocks, edge, width), F32),
            pltpu.VMEM(blocks.shape, blocks.dtype),
            pltpu.SemaphoreType.DMA((blocks.shape[0] // CHUNK,)),
        ],
        cost_estimate=pl.CostEstimate(
            flops=2 * blocks.shape[0] * edge * edge * width,
            bytes_accessed=2 * blocks.size + 2 * n_in * edge * width + 4 * n_out * out_blocks * edge * width,
            transcendentals=0,
        ),
        compiler_params=pltpu.CompilerParams(vmem_limit_bytes=16 << 20),
    )(table, pltpu.with_memory_space_constraint(blocks, pltpu.HBM), *pieces)


def spread(v):
    return jnp.broadcast_to(v, (SUB, LANES))


def eliminate(tiles, done):
    for g in range(BLOCK // STEP):
        k = lane = g * STEP
        head = tiles[g]
        rows = [spread(head[a : a + 1, :]) for a in range(STEP)]
        pivot = [[spread(head[a : a + 1, lane + b : lane + b + 1]) for b in range(a + 1)] for a in range(STEP)]
        rest = list(range(g + 1, len(tiles)))
        cols = {i: [spread(tiles[i][:, lane + a : lane + a + 1]) for a in range(STEP)] for i in rest}
        inverse = []
        for a in range(STEP):
            inverse.append(1.0 / pivot[a][a])
            for n in range(a + 1, STEP):
                ratio = pivot[n][a] * inverse[a]
                for b in range(a + 1, n + 1):
                    pivot[n][b] = pivot[n][b] - ratio * pivot[b][a]
                rows[n] = rows[n] - ratio * rows[a]
                for i in rest:
                    cols[i][n] = cols[i][n] - ratio * cols[i][a]
        for a in range(STEP):
            done[k + a : k + a + 1, :] = (rows[a] * lax.rsqrt(pivot[a][a]))[0:1, :]
        scaled = [rows[a] * inverse[a] for a in range(STEP)]
        for i in rest:
            terms = [cols[i][a] * scaled[a] for a in range(STEP)]
            while len(terms) > 1:
                terms = [terms[m] + terms[m + 1] for m in range(0, len(terms), 2)]
            tiles[i] = tiles[i] - terms[0]


def set_stage(work, stage, top):
    tile, offset = top // LANES * LANES, top % LANES
    part = work[top : top + BLOCK, tile : tile + LANES]
    if offset:
        part = pltpu.roll(part, BLOCK, 1)
    lanes = lax.broadcasted_iota(jnp.int32, (BLOCK, LANES), 1)
    unit = jnp.where(lanes == lax.broadcasted_iota(jnp.int32, (BLOCK, LANES), 0) + BLOCK, 1.0, 0.0)
    stage[...] = jnp.where(lanes < BLOCK, part, unit)


def apply_block(work, stage, done, factor, top):
    size = factor.shape[1]
    lanes = lax.broadcasted_iota(jnp.int32, (BLOCK, LANES), 1)
    inverse = jnp.where(lanes < BLOCK, 0.0, done[...])
    panel = work[top : top + BLOCK, :]
    upper = jnp.dot(
        inverse, jnp.concatenate([panel, panel], 0), precision=lax.Precision.HIGHEST, preferred_element_type=F32
    )
    rows = lax.broadcasted_iota(jnp.int32, (BLOCK, size), 0) + top
    keep = lax.broadcasted_iota(jnp.int32, (BLOCK, size), 1) >= rows
    head = jnp.where(keep, upper[:, :size], 0.0)
    factor[top : top + BLOCK, :] = head
    work[top : top + BLOCK, size:] = upper[:, size:]
    if top + BLOCK < size:
        low = (top + BLOCK) // LANES * LANES
        full = jnp.concatenate([head, upper[:, size:]], 1)
        take = lax.dot_general(
            head[:, low:],
            full[:, low:],
            (((0,), (0,)), ((), ())),
            precision=lax.Precision.HIGHEST,
            preferred_element_type=F32,
        )
        work[top + BLOCK :, low:] = work[top + BLOCK :, low:] - take[top + BLOCK - low :, :]
        set_stage(work, stage, top + BLOCK)


def factor_kernel(table, piece0, piece1, piece2, piece3, products, basis, factor, work, stage, done):
    edge, size = products.shape
    rows = size // (N_CORE * N_Y)
    my_core, my_y = table[3, 0] & (N_CORE - 1), table[3, 1] & (N_Y - 1)
    for k, piece in enumerate((piece0, piece1, piece2, piece3)):
        for side in range(N_CORE):
            at = (((my_core + side) & 1) * N_Y + ((my_y + k) & (N_Y - 1))) * rows
            work[pl.ds(pl.multiple_of(at, rows), rows), :size] = piece[side] * (1.0 / (N_ROW * N_COL * edge))
    work[:, size:] = products[...].T
    set_stage(work, stage, 0)

    def block(p, carry):
        eliminate([stage[i * SUB : (i + 1) * SUB, :] for i in range(BLOCK // SUB)], done)
        for q in range(size // BLOCK):
            pl.when(p == q)(lambda q=q: apply_block(work, stage, done, factor, q * BLOCK))
        return carry

    lax.fori_loop(0, size // BLOCK, block, 0)
    basis[...] = work[:, size:].T


def factor_and_basis(table, pieces, products):
    edge, size = products.shape
    vmem = pl.BlockSpec(memory_space=pltpu.VMEM)
    return pl.pallas_call(
        factor_kernel,
        out_shape=(jax.ShapeDtypeStruct((edge, size), F32), jax.ShapeDtypeStruct((size, size), F32)),
        in_specs=[pl.BlockSpec(memory_space=pltpu.SMEM)] + [vmem] * 5,
        out_specs=(vmem, vmem),
        scratch_shapes=[pltpu.VMEM((size, size + edge), F32)] + [pltpu.VMEM((BLOCK, LANES), F32)] * 2,
        compiler_params=pltpu.CompilerParams(vmem_limit_bytes=8 << 20),
        name="factor",
    )(table, *pieces, products)


def gram_pieces(products, r, c):
    width = products.shape[1]
    half, piece = width // N_CORE, width // (N_CORE * N_Y)
    my_core, my_y = r & (N_CORE - 1), c & (N_Y - 1)
    local = jnp.dot(products.T, products, precision=lax.Precision.HIGHEST, preferred_element_type=F32)
    mine = lax.dynamic_slice_in_dim(local, my_core * half, half, 0)
    other = lax.dynamic_slice_in_dim(local, (1 - my_core) * half, half, 0)
    pair = mine + to_core(other)
    parts = [lax.dynamic_slice_in_dim(pair, ((my_y + k) & (N_Y - 1)) * piece, piece, 0) for k in range(N_Y)]
    got = ring_sum([parts[0]] + [to_y(parts[k], k) for k in range(1, N_Y)])
    got = ring_sum([got] + [to_x(got, k) for k in range(1, N_X)])
    got = got + to_zl(got)
    got = ring_sum([got] + [to_z(got, k) for k in range(1, N_ZH)])
    both = jnp.stack([got, to_core(got)])
    return [both] + [to_y(both, -k) for k in range(1, N_Y)]


def body(blocks, block_rows, block_cols, counts, trials):
    r, c = lax.axis_index("row").astype(jnp.int32), lax.axis_index("col").astype(jnp.int32)
    slots = block_rows.shape[1]
    at = lax.broadcasted_iota(jnp.int32, (1, slots), 1)
    table = jnp.concatenate(
        [block_rows, block_cols, jnp.broadcast_to(counts, (1, slots)), jnp.where(at == 0, r, c)], 0
    )
    first = jnp.stack([trials, to_zl(trials)])
    zs = jnp.stack([trials] + [to_z(trials, -k) for k in range(1, N_ZH)])
    row_pieces = [first] + [to_y(first, -k) for k in range(1, N_Y)]
    col_pieces = [zs] + [to_x(zs, -k) for k in range(1, N_X)]
    outs = products_of(mirror_kernel, table, blocks[0], row_pieces, N_CORE * N_X, N_ZH)
    keep, send = outs[:N_X], outs[N_X:]
    col_pieces = col_pieces + [to_core(v) for v in col_pieces]
    row_outs = products_of(direct_kernel, table, blocks[0], col_pieces, N_Y, N_ZL)
    theirs = {k: to_core(send[k]) for k in (1, 3, 2, 0)}
    sent = {k: to_x(keep[k] + theirs[k], k) for k in (1, 3, 2)}
    got = ring_sum([keep[0] + theirs[0]] + [sent[k] for k in range(1, N_X)])
    rows = ring_sum([row_outs[0]] + [to_y(row_outs[k], k) for k in range(1, N_Y)])
    row_sum = rows[0] + to_zl(rows[1])
    col_sum = ring_sum([got[0]] + [to_z(got[k], k) for k in range(1, N_ZH)])
    products = row_sum + col_sum
    return factor_and_basis(table, gram_pieces(products, r, c), products)


def solution(mesh):
    return jax.shard_map(
        body,
        mesh=mesh,
        in_specs=(
            P("row", "col", None, None),
            P("row", "col"),
            P("row", "col"),
            P("row", "col"),
            P(("col", "row"), None),
        ),
        out_specs=(P(("col", "row"), None), P()),
        check_vma=False,
    )
```

```python
import jax
import jax.numpy as jnp
from jax import lax
from jax.experimental import pallas as pl
from jax.experimental.pallas import tpu as pltpu
from jax.sharding import PartitionSpec as P


N_ZH, N_X, N_CORE, N_ZL, N_Y = 4, 4, 2, 2, 4
N_ROW = N_ZH * N_X * N_CORE
N_COL = N_ZL * N_Y
F32 = jnp.float32
BLOCK, SUB, LANES = 64, 8, 128
STEP = SUB
CHUNK = 8
FIRST = 96


def row_at(z, x, c):
    return ((z % N_ZH) * N_X + x % N_X) * N_CORE + c


def col_at(zl, y):
    return zl * N_Y + y % N_Y


def row_pairs(move):
    return [(row_at(z, x, c), row_at(*move(z, x, c))) for z in range(N_ZH) for x in range(N_X) for c in range(N_CORE)]


def to_z(v, k):
    return lax.ppermute(v, "row", row_pairs(lambda z, x, c: (z + k, x, c)))


def to_x(v, k):
    return lax.ppermute(v, "row", row_pairs(lambda z, x, c: (z, x + k, c)))


def to_core(v):
    return lax.ppermute(v, "row", row_pairs(lambda z, x, c: (z, x, 1 - c)))


def to_y(v, k):
    return lax.ppermute(v, "col", [(col_at(zl, y), col_at(zl, y + k)) for zl in range(N_ZL) for y in range(N_Y)])


def to_zl(v):
    return lax.ppermute(v, "col", [(col_at(zl, y), col_at(1 - zl, y)) for zl in range(N_ZL) for y in range(N_Y)])


def ring_sum(parts):
    return (parts[0] + parts[2]) + (parts[1] + parts[3])


def clear(acc):
    def one(n, carry):
        acc[n] = jnp.zeros(acc.shape[1:], acc.dtype)
        return carry

    lax.fori_loop(0, acc.shape[0], one, 0)


def each(count, one):
    def step(n, carry):
        one(n)
        return carry

    lax.fori_loop(0, count, step, 0)


def slot_loop(table, blocks, tiles, sems, prepare, add):
    live = table[2, 0]
    chunks = (live + CHUNK - 1) // CHUNK

    def fetch(n):
        return pltpu.make_async_copy(
            blocks.at[pl.ds(n * CHUNK, CHUNK)], tiles.at[pl.ds(n * CHUNK, CHUNK)], sems.at[n]
        )

    def start(n, carry):
        fetch(n).start()
        return carry

    def visit(s):
        i, j = table[0, s], table[1, s]
        q = jnp.where(s < live, jnp.where(i == j, 0.5, 1.0), 0.0)
        tile = jnp.where(q > 0.0, tiles[s].astype(F32) * q, 0.0).astype(jnp.bfloat16)
        add(tile, i >> 5, j & (N_ROW - 1))

    def chunk(n, carry):
        fetch(n).wait()

        def group(g, inner):
            for u in range(4):
                visit(n * CHUNK + g * 4 + u)
            return inner

        return lax.fori_loop(0, CHUNK // 4, group, carry)

    lax.fori_loop(0, chunks, start, 0)
    prepare()
    lax.fori_loop(0, chunks, chunk, 0)


def row_spot(table, rp):
    c = table[3, 1]
    return ((rp - c) & 3) * N_ZL + ((rp ^ c) >> 2)


def col_spot(table, cp):
    r = table[3, 0]
    zk, xk, cx = ((cp >> 3) - (r >> 3)) & 3, ((cp >> 1) - (r >> 1)) & 3, (cp ^ r) & 1
    return cx * N_X * N_ZH + xk * N_ZH + zk


def mirror_kernel(table, blocks, *refs):
    pieces, outs, (vectors, acc, tiles, sems) = refs[:N_Y], refs[N_Y:-4], refs[-4:]

    def prepare():
        clear(acc)
        for k, piece in enumerate(pieces):
            vectors[k * N_ZL : (k + 1) * N_ZL] = piece[...]

    def add(tile, rp, cp):
        acc[col_spot(table, cp)] += lax.dot_general(
            tile, vectors[row_spot(table, rp)], (((0,), (0,)), ((), ())), preferred_element_type=F32
        )

    slot_loop(table, blocks, tiles, sems, prepare, add)
    part = N_X * N_ZH
    for k in range(N_CORE * N_X):

        def first(n, k=k):
            outs[k][n] = acc[k * N_ZH + n, :FIRST]

        each(N_ZH, first)
    for k in range(N_CORE):

        def second(n, k=k):
            outs[N_CORE * N_X + k][n] = acc[k * part + (n & (N_X - 1)) * N_ZH + n // N_X, FIRST:]

        each(part, second)


def direct_kernel(table, blocks, *refs):
    n = N_X + 1
    pieces, outs, (vectors, acc, tiles, sems) = refs[:n], refs[n:-4], refs[-4:]

    def prepare():
        clear(acc)
        at = 0
        for piece in pieces:
            vectors[at : at + piece.shape[0]] = piece[...]
            at += piece.shape[0]

    def add(tile, rp, cp):
        acc[row_spot(table, rp)] += jnp.dot(tile, vectors[col_spot(table, cp)], preferred_element_type=F32)

    slot_loop(table, blocks, tiles, sems, prepare, add)
    for k, out in enumerate(outs):

        def one(n, k=k, out=out):
            out[n] = acc[k * N_ZL + n]

        each(N_ZL, one)


def products_of(kernel, table, blocks, pieces, outs):
    edge, width = pieces[0].shape[1:]
    vmem = pl.BlockSpec(memory_space=pltpu.VMEM)
    n_in, n_acc = (sum(v.shape[0] for v in pieces), sum(n * rows for n, rows in outs) // edge)
    return pl.pallas_call(
        kernel,
        out_shape=tuple(jax.ShapeDtypeStruct((n, rows, width), F32) for n, rows in outs),
        in_specs=[pl.BlockSpec(memory_space=pltpu.SMEM), pl.BlockSpec(memory_space=pltpu.HBM)] + [vmem] * len(pieces),
        out_specs=(vmem,) * len(outs),
        scratch_shapes=[
            pltpu.VMEM((n_in, edge, width), jnp.bfloat16),
            pltpu.VMEM((n_acc, edge, width), F32),
            pltpu.VMEM(blocks.shape, blocks.dtype),
            pltpu.SemaphoreType.DMA((blocks.shape[0] // CHUNK,)),
        ],
        cost_estimate=pl.CostEstimate(
            flops=2 * blocks.shape[0] * edge * edge * width,
            bytes_accessed=2 * blocks.size + 2 * n_in * edge * width + 4 * n_acc * edge * width,
            transcendentals=0,
        ),
        compiler_params=pltpu.CompilerParams(vmem_limit_bytes=14 << 20),
    )(table, pltpu.with_memory_space_constraint(blocks, pltpu.HBM), *pieces)


def spread(v):
    return jnp.broadcast_to(v, (SUB, LANES))


def eliminate(tiles, done):
    for g in range(BLOCK // STEP):
        k = lane = g * STEP
        head = tiles[g]
        rows = [spread(head[a : a + 1, :]) for a in range(STEP)]
        pivot = [[spread(head[a : a + 1, lane + b : lane + b + 1]) for b in range(a + 1)] for a in range(STEP)]
        rest = list(range(g + 1, len(tiles)))
        cols = {i: [spread(tiles[i][:, lane + a : lane + a + 1]) for a in range(STEP)] for i in rest}
        inverse = []
        for a in range(STEP):
            inverse.append(1.0 / pivot[a][a])
            for n in range(a + 1, STEP):
                ratio = pivot[n][a] * inverse[a]
                for b in range(a + 1, n + 1):
                    pivot[n][b] = pivot[n][b] - ratio * pivot[b][a]
                rows[n] = rows[n] - ratio * rows[a]
                for i in rest:
                    cols[i][n] = cols[i][n] - ratio * cols[i][a]
        for a in range(STEP):
            done[k + a : k + a + 1, :] = (rows[a] * lax.rsqrt(pivot[a][a]))[0:1, :]
        scaled = [rows[a] * inverse[a] for a in range(STEP)]
        for i in rest:
            terms = [cols[i][a] * scaled[a] for a in range(STEP)]
            while len(terms) > 1:
                terms = [terms[m] + terms[m + 1] for m in range(0, len(terms), 2)]
            tiles[i] = tiles[i] - terms[0]


def set_stage(work, stage, top):
    tile, offset = top // LANES * LANES, top % LANES
    part = work[top : top + BLOCK, tile : tile + LANES]
    if offset:
        part = pltpu.roll(part, BLOCK, 1)
    lanes = lax.broadcasted_iota(jnp.int32, (BLOCK, LANES), 1)
    unit = jnp.where(lanes == lax.broadcasted_iota(jnp.int32, (BLOCK, LANES), 0) + BLOCK, 1.0, 0.0)
    stage[...] = jnp.where(lanes < BLOCK, part, unit)


def apply_block(work, stage, done, factor, top):
    size = factor.shape[1]
    lanes = lax.broadcasted_iota(jnp.int32, (BLOCK, LANES), 1)
    inverse = jnp.where(lanes < BLOCK, 0.0, done[...])
    panel = work[top : top + BLOCK, :]
    upper = jnp.dot(
        inverse, jnp.concatenate([panel, panel], 0), precision=lax.Precision.HIGHEST, preferred_element_type=F32
    )
    rows = lax.broadcasted_iota(jnp.int32, (BLOCK, size), 0) + top
    keep = lax.broadcasted_iota(jnp.int32, (BLOCK, size), 1) >= rows
    head = jnp.where(keep, upper[:, :size], 0.0)
    factor[top : top + BLOCK, :] = head
    work[top : top + BLOCK, size:] = upper[:, size:]
    if top + BLOCK < size:
        low = (top + BLOCK) // LANES * LANES
        full = jnp.concatenate([head, upper[:, size:]], 1)
        take = lax.dot_general(
            head[:, low:],
            full[:, low:],
            (((0,), (0,)), ((), ())),
            precision=lax.Precision.HIGHEST,
            preferred_element_type=F32,
        )
        work[top + BLOCK :, low:] = work[top + BLOCK :, low:] - take[top + BLOCK - low :, :]
        set_stage(work, stage, top + BLOCK)


def factor_kernel(table, piece0, piece1, piece2, piece3, products, basis, factor, work, stage, done):
    edge, size = products.shape
    rows = size // (N_CORE * N_Y)
    my_core, my_y = table[3, 0] & (N_CORE - 1), table[3, 1] & (N_Y - 1)
    for k, piece in enumerate((piece0, piece1, piece2, piece3)):
        for side in range(N_CORE):
            at = (((my_core + side) & 1) * N_Y + ((my_y + k) & (N_Y - 1))) * rows
            work[pl.ds(pl.multiple_of(at, rows), rows), :size] = piece[side] * (1.0 / (N_ROW * N_COL * edge))
    work[:, size:] = products[...].T
    set_stage(work, stage, 0)

    def block(p, carry):
        eliminate([stage[i * SUB : (i + 1) * SUB, :] for i in range(BLOCK // SUB)], done)
        for q in range(size // BLOCK):
            pl.when(p == q)(lambda q=q: apply_block(work, stage, done, factor, q * BLOCK))
        return carry

    lax.fori_loop(0, size // BLOCK, block, 0)
    basis[...] = work[:, size:].T


def factor_and_basis(table, pieces, products):
    edge, size = products.shape
    vmem = pl.BlockSpec(memory_space=pltpu.VMEM)
    return pl.pallas_call(
        factor_kernel,
        out_shape=(jax.ShapeDtypeStruct((edge, size), F32), jax.ShapeDtypeStruct((size, size), F32)),
        in_specs=[pl.BlockSpec(memory_space=pltpu.SMEM)] + [vmem] * 5,
        out_specs=(vmem, vmem),
        scratch_shapes=[pltpu.VMEM((size, size + edge), F32)] + [pltpu.VMEM((BLOCK, LANES), F32)] * 2,
        compiler_params=pltpu.CompilerParams(vmem_limit_bytes=8 << 20),
        name="factor",
    )(table, *pieces, products)


def gram_pieces(products, r, c):
    width = products.shape[1]
    half, piece = width // N_CORE, width // (N_CORE * N_Y)
    my_core, my_y = r & (N_CORE - 1), c & (N_Y - 1)
    local = jnp.dot(products.T, products, precision=lax.Precision.HIGHEST, preferred_element_type=F32)
    mine = lax.dynamic_slice_in_dim(local, my_core * half, half, 0)
    other = lax.dynamic_slice_in_dim(local, (1 - my_core) * half, half, 0)
    pair = mine + to_core(other)
    parts = [lax.dynamic_slice_in_dim(pair, ((my_y + k) & (N_Y - 1)) * piece, piece, 0) for k in range(N_Y)]
    got = ring_sum([parts[0]] + [to_y(parts[k], k) for k in range(1, N_Y)])
    got = ring_sum([got] + [to_x(got, k) for k in range(1, N_X)])
    got = got + to_zl(got)
    got = ring_sum([got] + [to_z(got, k) for k in range(1, N_ZH)])
    both = jnp.stack([got, to_core(got)])
    return [both] + [to_y(both, -k) for k in range(1, N_Y)]


def body(blocks, block_rows, block_cols, counts, trials):
    edge, _ = trials.shape
    r, c = lax.axis_index("row").astype(jnp.int32), lax.axis_index("col").astype(jnp.int32)
    slots = block_rows.shape[1]
    at = lax.broadcasted_iota(jnp.int32, (1, slots), 1)
    table = jnp.concatenate(
        [block_rows, block_cols, jnp.broadcast_to(counts, (1, slots)), jnp.where(at == 0, r, c)], 0
    )
    first = jnp.stack([trials, to_zl(trials)])
    zs = jnp.stack([trials] + [to_z(trials, -k) for k in range(1, N_ZH)])
    row_pieces = [first] + [to_y(first, -k) for k in range(1, N_Y)]
    col_pieces = [zs] + [to_x(zs, -k) for k in range(1, N_X)]
    outs = products_of(
        mirror_kernel,
        table,
        blocks[0],
        row_pieces,
        [(N_ZH, FIRST)] * (N_CORE * N_X) + [(N_X * N_ZH, edge - FIRST)] * N_CORE,
    )
    keep, send, (keep_b, send_b) = outs[:N_X], outs[N_X : 2 * N_X], outs[2 * N_X :]
    col_pieces = col_pieces + [to_core(jnp.concatenate(col_pieces, 0))]
    row_outs = products_of(direct_kernel, table, blocks[0], col_pieces, [(N_ZL, edge)] * N_Y)
    theirs = {k: to_core(send[k]) for k in (1, 3, 2, 0)}
    pair = {k: keep[k] + theirs[k] for k in (1, 3, 2)}
    sent = {k: to_x(pair[k], k) for k in (1, 3, 2)}
    got = ring_sum([keep[0] + theirs[0]] + [sent[k] for k in range(1, N_X)])
    both = keep_b + to_core(send_b)
    parts = [both[k * N_X : (k + 1) * N_X] for k in range(N_ZH)]
    got_b = ring_sum([parts[0]] + [to_z(parts[k], k) for k in range(1, N_ZH)])
    rows = ring_sum([row_outs[0]] + [to_y(row_outs[k], k) for k in range(1, N_Y)])
    row_sum = rows[0] + to_zl(rows[1])
    sum_b = ring_sum([got_b[0]] + [to_x(got_b[k], k) for k in range(1, N_X)])
    sum_a = ring_sum([got[0]] + [to_z(got[k], k) for k in range(1, N_ZH)])
    col_sum = jnp.concatenate([sum_a, sum_b], 0)
    products = row_sum + col_sum
    return factor_and_basis(table, gram_pieces(products, r, c), products)


def solution(mesh):
    return jax.shard_map(
        body,
        mesh=mesh,
        in_specs=(
            P("row", "col", None, None),
            P("row", "col"),
            P("row", "col"),
            P("row", "col"),
            P(("col", "row"), None),
        ),
        out_specs=(P(("col", "row"), None), P()),
        check_vma=False,
    )
```

```python
import jax
import jax.numpy as jnp
from jax import lax
from jax.experimental import pallas as pl
from jax.experimental.pallas import tpu as pltpu
from jax.sharding import PartitionSpec as P


N_ZH, N_X, N_CORE, N_ZL, N_Y = 4, 4, 2, 2, 4
N_ROW = N_ZH * N_X * N_CORE
N_COL = N_ZL * N_Y
F32 = jnp.float32
BLOCK, SUB, LANES = 64, 8, 128
STEP = SUB
CHUNK = 8


def row_at(z, x, c):
    return ((z % N_ZH) * N_X + x % N_X) * N_CORE + c


def col_at(zl, y):
    return zl * N_Y + y % N_Y


def row_pairs(move):
    return [(row_at(z, x, c), row_at(*move(z, x, c))) for z in range(N_ZH) for x in range(N_X) for c in range(N_CORE)]


def to_z(v, k):
    return lax.ppermute(v, "row", row_pairs(lambda z, x, c: (z + (1 - 2 * c) * k, x, c)))


def to_x(v, k):
    return lax.ppermute(v, "row", row_pairs(lambda z, x, c: (z, x + (1 - 2 * c) * k, c)))


def to_core(v):
    return lax.ppermute(v, "row", row_pairs(lambda z, x, c: (z, x, 1 - c)))


def to_y(v, k):
    return lax.ppermute(v, "col", [(col_at(zl, y), col_at(zl, y + k)) for zl in range(N_ZL) for y in range(N_Y)])


def to_zl(v):
    return lax.ppermute(v, "col", [(col_at(zl, y), col_at(1 - zl, y)) for zl in range(N_ZL) for y in range(N_Y)])


def ring_sum(parts):
    return (parts[0] + parts[2]) + (parts[1] + parts[3])


def clear(acc):
    def one(n, carry):
        acc[n] = jnp.zeros(acc.shape[1:], acc.dtype)
        return carry

    lax.fori_loop(0, acc.shape[0], one, 0)


def hand_out(acc, outs):
    for k, out in enumerate(outs):
        size = out.shape[0]

        def one(n, carry):
            out[n] = acc[k * size + n]
            return carry

        lax.fori_loop(0, size, one, 0)


def slot_loop(table, blocks, tiles, sems, prepare, add):
    live = table[2, 0]
    chunks = (live + CHUNK - 1) // CHUNK

    def fetch(n):
        return pltpu.make_async_copy(
            blocks.at[pl.ds(n * CHUNK, CHUNK)], tiles.at[pl.ds(n * CHUNK, CHUNK)], sems.at[n]
        )

    def start(n, carry):
        fetch(n).start()
        return carry

    def visit(s):
        i, j = table[0, s], table[1, s]
        q = jnp.where(s < live, jnp.where(i == j, 0.5, 1.0), 0.0)
        tile = jnp.where(q > 0.0, tiles[s].astype(F32) * q, 0.0).astype(jnp.bfloat16)
        add(tile, i >> 5, j & (N_ROW - 1))

    def chunk(n, carry):
        fetch(n).wait()

        def group(g, inner):
            for u in range(4):
                visit(n * CHUNK + g * 4 + u)
            return inner

        return lax.fori_loop(0, CHUNK // 4, group, carry)

    lax.fori_loop(0, chunks, start, 0)
    prepare()
    lax.fori_loop(0, chunks, chunk, 0)


def row_spot(table, rp):
    c = table[3, 1]
    return ((rp - c) & 3) * N_ZL + ((rp ^ c) >> 2)


def col_spot(table, cp):
    r = table[3, 0]
    way = 1 - 2 * (cp & 1)
    zk, xk, cx = (((cp >> 3) - (r >> 3)) * way) & 3, (((cp >> 1) - (r >> 1)) * way) & 3, (cp ^ r) & 1
    return cx * N_X * N_ZH + xk * N_ZH + zk


def mirror_kernel(table, blocks, *refs):
    pieces, outs, (vectors, acc, tiles, sems) = refs[:N_Y], refs[N_Y:-4], refs[-4:]

    def prepare():
        clear(acc)
        for k, piece in enumerate(pieces):
            vectors[k * N_ZL : (k + 1) * N_ZL] = piece[...]

    def add(tile, rp, cp):
        acc[col_spot(table, cp)] += lax.dot_general(
            tile, vectors[row_spot(table, rp)], (((0,), (0,)), ((), ())), preferred_element_type=F32
        )

    slot_loop(table, blocks, tiles, sems, prepare, add)
    hand_out(acc, outs)


def direct_kernel(table, blocks, *refs):
    n = N_CORE * N_X
    pieces, outs, (vectors, acc, tiles, sems) = refs[:n], refs[n:-4], refs[-4:]

    def prepare():
        clear(acc)
        for k, piece in enumerate(pieces):
            vectors[k * N_ZH : (k + 1) * N_ZH] = piece[...]

    def add(tile, rp, cp):
        acc[row_spot(table, rp)] += jnp.dot(tile, vectors[col_spot(table, cp)], preferred_element_type=F32)

    slot_loop(table, blocks, tiles, sems, prepare, add)
    hand_out(acc, outs)


def products_of(kernel, table, blocks, pieces, n_out, out_blocks):
    edge, width = pieces[0].shape[1:]
    vmem = pl.BlockSpec(memory_space=pltpu.VMEM)
    n_in = len(pieces) * pieces[0].shape[0]
    return pl.pallas_call(
        kernel,
        out_shape=(jax.ShapeDtypeStruct((out_blocks, edge, width), F32),) * n_out,
        in_specs=[pl.BlockSpec(memory_space=pltpu.SMEM), pl.BlockSpec(memory_space=pltpu.HBM)] + [vmem] * len(pieces),
        out_specs=(vmem,) * n_out,
        scratch_shapes=[
            pltpu.VMEM((n_in, edge, width), jnp.bfloat16),
            pltpu.VMEM((n_out * out_blocks, edge, width), F32),
            pltpu.VMEM(blocks.shape, blocks.dtype),
            pltpu.SemaphoreType.DMA((blocks.shape[0] // CHUNK,)),
        ],
        cost_estimate=pl.CostEstimate(
            flops=2 * blocks.shape[0] * edge * edge * width,
            bytes_accessed=2 * blocks.size + 2 * n_in * edge * width + 4 * n_out * out_blocks * edge * width,
            transcendentals=0,
        ),
        compiler_params=pltpu.CompilerParams(vmem_limit_bytes=16 << 20),
    )(table, pltpu.with_memory_space_constraint(blocks, pltpu.HBM), *pieces)


def spread(v):
    return jnp.broadcast_to(v, (SUB, LANES))


def eliminate(tiles, done):
    for g in range(BLOCK // STEP):
        k = lane = g * STEP
        head = tiles[g]
        rows = [spread(head[a : a + 1, :]) for a in range(STEP)]
        pivot = [[spread(head[a : a + 1, lane + b : lane + b + 1]) for b in range(a + 1)] for a in range(STEP)]
        rest = list(range(g + 1, len(tiles)))
        cols = {i: [spread(tiles[i][:, lane + a : lane + a + 1]) for a in range(STEP)] for i in rest}
        inverse = []
        for a in range(STEP):
            inverse.append(1.0 / pivot[a][a])
            for n in range(a + 1, STEP):
                ratio = pivot[n][a] * inverse[a]
                for b in range(a + 1, n + 1):
                    pivot[n][b] = pivot[n][b] - ratio * pivot[b][a]
                rows[n] = rows[n] - ratio * rows[a]
                for i in rest:
                    cols[i][n] = cols[i][n] - ratio * cols[i][a]
        for a in range(STEP):
            done[k + a : k + a + 1, :] = (rows[a] * lax.rsqrt(pivot[a][a]))[0:1, :]
        scaled = [rows[a] * inverse[a] for a in range(STEP)]
        for i in rest:
            terms = [cols[i][a] * scaled[a] for a in range(STEP)]
            while len(terms) > 1:
                terms = [terms[m] + terms[m + 1] for m in range(0, len(terms), 2)]
            tiles[i] = tiles[i] - terms[0]


def set_stage(work, stage, top):
    tile, offset = top // LANES * LANES, top % LANES
    part = work[top : top + BLOCK, tile : tile + LANES]
    if offset:
        part = pltpu.roll(part, BLOCK, 1)
    lanes = lax.broadcasted_iota(jnp.int32, (BLOCK, LANES), 1)
    unit = jnp.where(lanes == lax.broadcasted_iota(jnp.int32, (BLOCK, LANES), 0) + BLOCK, 1.0, 0.0)
    stage[...] = jnp.where(lanes < BLOCK, part, unit)


def apply_block(work, stage, done, factor, top):
    size = factor.shape[1]
    lanes = lax.broadcasted_iota(jnp.int32, (BLOCK, LANES), 1)
    inverse = jnp.where(lanes < BLOCK, 0.0, done[...])
    panel = work[top : top + BLOCK, :]
    upper = jnp.dot(
        inverse, jnp.concatenate([panel, panel], 0), precision=lax.Precision.HIGHEST, preferred_element_type=F32
    )
    rows = lax.broadcasted_iota(jnp.int32, (BLOCK, size), 0) + top
    keep = lax.broadcasted_iota(jnp.int32, (BLOCK, size), 1) >= rows
    head = jnp.where(keep, upper[:, :size], 0.0)
    factor[top : top + BLOCK, :] = head
    work[top : top + BLOCK, size:] = upper[:, size:]
    if top + BLOCK < size:
        low = (top + BLOCK) // LANES * LANES
        full = jnp.concatenate([head, upper[:, size:]], 1)
        take = lax.dot_general(
            head[:, low:],
            full[:, low:],
            (((0,), (0,)), ((), ())),
            precision=lax.Precision.HIGHEST,
            preferred_element_type=F32,
        )
        work[top + BLOCK :, low:] = work[top + BLOCK :, low:] - take[top + BLOCK - low :, :]
        set_stage(work, stage, top + BLOCK)


def factor_kernel(table, piece0, piece1, piece2, piece3, products, basis, factor, work, stage, done):
    edge, size = products.shape
    rows = size // (N_CORE * N_Y)
    my_core, my_y = table[3, 0] & (N_CORE - 1), table[3, 1] & (N_Y - 1)
    for k, piece in enumerate((piece0, piece1, piece2, piece3)):
        for side in range(N_CORE):
            at = (((my_core + side) & 1) * N_Y + ((my_y + k) & (N_Y - 1))) * rows
            work[pl.ds(pl.multiple_of(at, rows), rows), :size] = piece[side] * (1.0 / (N_ROW * N_COL * edge))
    work[:, size:] = products[...].T
    set_stage(work, stage, 0)

    def block(p, carry):
        eliminate([stage[i * SUB : (i + 1) * SUB, :] for i in range(BLOCK // SUB)], done)
        for q in range(size // BLOCK):
            pl.when(p == q)(lambda q=q: apply_block(work, stage, done, factor, q * BLOCK))
        return carry

    lax.fori_loop(0, size // BLOCK, block, 0)
    basis[...] = work[:, size:].T


def factor_and_basis(table, pieces, products):
    edge, size = products.shape
    vmem = pl.BlockSpec(memory_space=pltpu.VMEM)
    return pl.pallas_call(
        factor_kernel,
        out_shape=(jax.ShapeDtypeStruct((edge, size), F32), jax.ShapeDtypeStruct((size, size), F32)),
        in_specs=[pl.BlockSpec(memory_space=pltpu.SMEM)] + [vmem] * 5,
        out_specs=(vmem, vmem),
        scratch_shapes=[pltpu.VMEM((size, size + edge), F32)] + [pltpu.VMEM((BLOCK, LANES), F32)] * 2,
        compiler_params=pltpu.CompilerParams(vmem_limit_bytes=8 << 20),
        name="factor",
    )(table, *pieces, products)


def gram_pieces(products, r, c):
    width = products.shape[1]
    half, piece = width // N_CORE, width // (N_CORE * N_Y)
    my_core, my_y = r & (N_CORE - 1), c & (N_Y - 1)
    local = jnp.dot(products.T, products, precision=lax.Precision.HIGHEST, preferred_element_type=F32)
    mine = lax.dynamic_slice_in_dim(local, my_core * half, half, 0)
    other = lax.dynamic_slice_in_dim(local, (1 - my_core) * half, half, 0)
    pair = mine + to_core(other)
    parts = [lax.dynamic_slice_in_dim(pair, ((my_y + k) & (N_Y - 1)) * piece, piece, 0) for k in range(N_Y)]
    got = ring_sum([parts[0]] + [to_y(parts[k], k) for k in range(1, N_Y)])
    got = ring_sum([got] + [to_x(got, k) for k in range(1, N_X)])
    got = got + to_zl(got)
    got = ring_sum([got] + [to_z(got, k) for k in range(1, N_ZH)])
    both = jnp.stack([got, to_core(got)])
    return [both] + [to_y(both, -k) for k in range(1, N_Y)]


def body(blocks, block_rows, block_cols, counts, trials):
    r, c = lax.axis_index("row").astype(jnp.int32), lax.axis_index("col").astype(jnp.int32)
    slots = block_rows.shape[1]
    at = lax.broadcasted_iota(jnp.int32, (1, slots), 1)
    table = jnp.concatenate(
        [block_rows, block_cols, jnp.broadcast_to(counts, (1, slots)), jnp.where(at == 0, r, c)], 0
    )
    first = jnp.stack([trials, to_zl(trials)])
    zs = jnp.stack([trials] + [to_z(trials, -k) for k in range(1, N_ZH)])
    row_pieces = [first] + [to_y(first, -k) for k in range(1, N_Y)]
    col_pieces = [zs] + [to_x(zs, -k) for k in range(1, N_X)]
    outs = products_of(mirror_kernel, table, blocks[0], row_pieces, N_CORE * N_X, N_ZH)
    keep, send = outs[:N_X], outs[N_X:]
    col_pieces = col_pieces + [to_core(v) for v in col_pieces]
    row_outs = products_of(direct_kernel, table, blocks[0], col_pieces, N_Y, N_ZL)
    theirs = {k: to_core(send[k]) for k in (1, 3, 2, 0)}
    sent = {k: to_x(keep[k] + theirs[k], k) for k in (1, 3, 2)}
    got = ring_sum([keep[0] + theirs[0]] + [sent[k] for k in range(1, N_X)])
    rows = ring_sum([row_outs[0]] + [to_y(row_outs[k], k) for k in range(1, N_Y)])
    row_sum = rows[0] + to_zl(rows[1])
    col_sum = ring_sum([got[0]] + [to_z(got[k], k) for k in range(1, N_ZH)])
    products = row_sum + col_sum
    return factor_and_basis(table, gram_pieces(products, r, c), products)


def solution(mesh):
    return jax.shard_map(
        body,
        mesh=mesh,
        in_specs=(
            P("row", "col", None, None),
            P("row", "col"),
            P("row", "col"),
            P("row", "col"),
            P(("col", "row"), None),
        ),
        out_specs=(P(("col", "row"), None), P()),
        check_vma=False,
    )
```

```python
import math

import jax
import jax.numpy as jnp
from jax import lax
from jax.experimental import pallas as pl
from jax.experimental.pallas import tpu as pltpu
from jax.sharding import PartitionSpec as P


N_ZH, N_X, N_CORE, N_ZL, N_Y = 4, 4, 2, 2, 4
N_ROW = N_ZH * N_X * N_CORE
N_COL = N_ZL * N_Y
F32 = jnp.float32
BLOCK, SUB, LANES = 64, 8, 128
STEP = SUB
CHUNK = 8
FIRST = 104


def row_at(z, x, c):
    return ((z % N_ZH) * N_X + x % N_X) * N_CORE + c


def col_at(zl, y):
    return zl * N_Y + y % N_Y


def row_pairs(move):
    return [(row_at(z, x, c), row_at(*move(z, x, c))) for z in range(N_ZH) for x in range(N_X) for c in range(N_CORE)]


def to_z(v, k):
    return lax.ppermute(v, "row", row_pairs(lambda z, x, c: (z + k, x, c)))


def to_x(v, k):
    return lax.ppermute(v, "row", row_pairs(lambda z, x, c: (z, x + k, c)))


def to_core(v):
    return lax.ppermute(v, "row", row_pairs(lambda z, x, c: (z, x, 1 - c)))


def to_y(v, k):
    return lax.ppermute(v, "col", [(col_at(zl, y), col_at(zl, y + k)) for zl in range(N_ZL) for y in range(N_Y)])


def to_zl(v):
    return lax.ppermute(v, "col", [(col_at(zl, y), col_at(1 - zl, y)) for zl in range(N_ZL) for y in range(N_Y)])


def ring_sum(parts):
    return (parts[0] + parts[2]) + (parts[1] + parts[3])


def clear(acc):
    def one(n, carry):
        acc[n] = jnp.zeros(acc.shape[1:], acc.dtype)
        return carry

    lax.fori_loop(0, acc.shape[0], one, 0)


def each(count, one):
    def step(n, carry):
        one(n)
        return carry

    lax.fori_loop(0, count, step, 0)


def slot_loop(table, blocks, tiles, sems, prepare, add):
    live = table[2, 0]
    chunks = (live + CHUNK - 1) // CHUNK

    def fetch(n):
        return pltpu.make_async_copy(
            blocks.at[pl.ds(n * CHUNK, CHUNK)], tiles.at[pl.ds(n * CHUNK, CHUNK)], sems.at[n]
        )

    def start(n, carry):
        fetch(n).start()
        return carry

    def visit(s):
        i, j = table[0, s], table[1, s]
        q = jnp.where(s < live, jnp.where(i == j, 0.5, 1.0), 0.0)
        tile = jnp.where(q > 0.0, tiles[s].astype(F32) * q, 0.0).astype(jnp.bfloat16)
        add(tile, i >> 5, j & (N_ROW - 1))

    def chunk(n, carry):
        fetch(n).wait()

        def group(g, inner):
            for u in range(4):
                visit(n * CHUNK + g * 4 + u)
            return inner

        return lax.fori_loop(0, CHUNK // 4, group, carry)

    lax.fori_loop(0, chunks, start, 0)
    prepare()
    lax.fori_loop(0, chunks, chunk, 0)


def row_spot(table, rp):
    c = table[3, 1]
    return ((rp - c) & 3) * N_ZL + ((rp ^ c) >> 2)


def col_spot(table, cp):
    r = table[3, 0]
    zk, xk, cx = ((cp >> 3) - (r >> 3)) & 3, ((cp >> 1) - (r >> 1)) & 3, (cp ^ r) & 1
    return cx * N_X * N_ZH + xk * N_ZH + zk


def mirror_kernel(table, blocks, *refs):
    pieces, outs, (vectors, acc, tiles, sems) = refs[:N_Y], refs[N_Y:-4], refs[-4:]

    def prepare():
        clear(acc)
        for k, piece in enumerate(pieces):
            vectors[k * N_ZL : (k + 1) * N_ZL] = piece[...]

    def add(tile, rp, cp):
        acc[col_spot(table, cp)] += lax.dot_general(
            tile, vectors[row_spot(table, rp)], (((0,), (0,)), ((), ())), preferred_element_type=F32
        )

    slot_loop(table, blocks, tiles, sems, prepare, add)
    part, edge = N_X * N_ZH, acc.shape[1]
    for side in range(N_CORE):
        flat, ones, threes = outs[side * 3 : side * 3 + 3]

        def first(n, side=side, flat=flat, ones=ones, threes=threes):
            base = side * part + n
            ones[n] = acc[base + N_ZH, :FIRST]
            threes[n] = acc[base + 3 * N_ZH, :FIRST]
            flat[pl.ds(pl.multiple_of(n * FIRST, SUB), FIRST), :] = acc[base + 2 * N_ZH, :FIRST]
            flat[pl.ds(pl.multiple_of((N_ZH + n) * FIRST, SUB), FIRST), :] = acc[base, :FIRST]

        def second(n, side=side, flat=flat):
            at = pl.multiple_of(2 * N_ZH * FIRST + n * (edge - FIRST), SUB)
            flat[pl.ds(at, edge - FIRST), :] = acc[side * part + (n & (N_X - 1)) * N_ZH + n // N_X, FIRST:]

        each(N_ZH, first)
        each(part, second)


def direct_kernel(table, blocks, *refs):
    n = N_CORE * N_X
    pieces, outs, (vectors, acc, tiles, sems) = refs[:n], refs[n:-4], refs[-4:]

    def prepare():
        clear(acc)
        at = 0
        for piece in pieces:
            vectors[at : at + piece.shape[0]] = piece[...]
            at += piece.shape[0]

    def add(tile, rp, cp):
        acc[row_spot(table, rp)] += jnp.dot(tile, vectors[col_spot(table, cp)], preferred_element_type=F32)

    slot_loop(table, blocks, tiles, sems, prepare, add)
    for k, out in enumerate(outs):

        def one(n, k=k, out=out):
            out[n] = acc[k * N_ZL + n]

        each(N_ZL, one)


def products_of(kernel, table, blocks, pieces, outs):
    edge, width = pieces[0].shape[1:]
    vmem = pl.BlockSpec(memory_space=pltpu.VMEM)
    n_in, n_acc = (sum(v.shape[0] for v in pieces), sum(math.prod(v) for v in outs) // edge)
    return pl.pallas_call(
        kernel,
        out_shape=tuple(jax.ShapeDtypeStruct(v + (width,), F32) for v in outs),
        in_specs=[pl.BlockSpec(memory_space=pltpu.SMEM), pl.BlockSpec(memory_space=pltpu.HBM)] + [vmem] * len(pieces),
        out_specs=(vmem,) * len(outs),
        scratch_shapes=[
            pltpu.VMEM((n_in, edge, width), jnp.bfloat16),
            pltpu.VMEM((n_acc, edge, width), F32),
            pltpu.VMEM(blocks.shape, blocks.dtype),
            pltpu.SemaphoreType.DMA((blocks.shape[0] // CHUNK,)),
        ],
        cost_estimate=pl.CostEstimate(
            flops=2 * blocks.shape[0] * edge * edge * width,
            bytes_accessed=2 * blocks.size + 2 * n_in * edge * width + 4 * n_acc * edge * width,
            transcendentals=0,
        ),
        compiler_params=pltpu.CompilerParams(vmem_limit_bytes=14 << 20),
    )(table, pltpu.with_memory_space_constraint(blocks, pltpu.HBM), *pieces)


def spread(v):
    return jnp.broadcast_to(v, (SUB, LANES))


def eliminate(tiles, done):
    for g in range(BLOCK // STEP):
        k = lane = g * STEP
        head = tiles[g]
        rows = [spread(head[a : a + 1, :]) for a in range(STEP)]
        pivot = [[spread(head[a : a + 1, lane + b : lane + b + 1]) for b in range(a + 1)] for a in range(STEP)]
        rest = list(range(g + 1, len(tiles)))
        cols = {i: [spread(tiles[i][:, lane + a : lane + a + 1]) for a in range(STEP)] for i in rest}
        inverse = []
        for a in range(STEP):
            inverse.append(1.0 / pivot[a][a])
            for n in range(a + 1, STEP):
                ratio = pivot[n][a] * inverse[a]
                for b in range(a + 1, n + 1):
                    pivot[n][b] = pivot[n][b] - ratio * pivot[b][a]
                rows[n] = rows[n] - ratio * rows[a]
                for i in rest:
                    cols[i][n] = cols[i][n] - ratio * cols[i][a]
        for a in range(STEP):
            done[k + a : k + a + 1, :] = (rows[a] * lax.rsqrt(pivot[a][a]))[0:1, :]
        scaled = [rows[a] * inverse[a] for a in range(STEP)]
        for i in rest:
            terms = [cols[i][a] * scaled[a] for a in range(STEP)]
            while len(terms) > 1:
                terms = [terms[m] + terms[m + 1] for m in range(0, len(terms), 2)]
            tiles[i] = tiles[i] - terms[0]


def set_stage(work, stage, top):
    tile, offset = top // LANES * LANES, top % LANES
    part = work[top : top + BLOCK, tile : tile + LANES]
    if offset:
        part = pltpu.roll(part, BLOCK, 1)
    lanes = lax.broadcasted_iota(jnp.int32, (BLOCK, LANES), 1)
    unit = jnp.where(lanes == lax.broadcasted_iota(jnp.int32, (BLOCK, LANES), 0) + BLOCK, 1.0, 0.0)
    stage[...] = jnp.where(lanes < BLOCK, part, unit)


def apply_block(work, stage, done, factor, top):
    size = factor.shape[1]
    lanes = lax.broadcasted_iota(jnp.int32, (BLOCK, LANES), 1)
    inverse = jnp.where(lanes < BLOCK, 0.0, done[...])
    panel = work[top : top + BLOCK, :]
    upper = jnp.dot(
        inverse, jnp.concatenate([panel, panel], 0), precision=lax.Precision.HIGHEST, preferred_element_type=F32
    )
    rows = lax.broadcasted_iota(jnp.int32, (BLOCK, size), 0) + top
    keep = lax.broadcasted_iota(jnp.int32, (BLOCK, size), 1) >= rows
    head = jnp.where(keep, upper[:, :size], 0.0)
    factor[top : top + BLOCK, :] = head
    work[top : top + BLOCK, size:] = upper[:, size:]
    if top + BLOCK < size:
        low = (top + BLOCK) // LANES * LANES
        full = jnp.concatenate([head, upper[:, size:]], 1)
        take = lax.dot_general(
            head[:, low:],
            full[:, low:],
            (((0,), (0,)), ((), ())),
            precision=lax.Precision.HIGHEST,
            preferred_element_type=F32,
        )
        work[top + BLOCK :, low:] = work[top + BLOCK :, low:] - take[top + BLOCK - low :, :]
        set_stage(work, stage, top + BLOCK)


def factor_kernel(table, piece0, piece1, piece2, piece3, products, basis, factor, work, stage, done):
    edge, size = products.shape
    rows = size // (N_CORE * N_Y)
    my_core, my_y = table[3, 0] & (N_CORE - 1), table[3, 1] & (N_Y - 1)
    for k, piece in enumerate((piece0, piece1, piece2, piece3)):
        for side in range(N_CORE):
            at = (((my_core + side) & 1) * N_Y + ((my_y + k) & (N_Y - 1))) * rows
            work[pl.ds(pl.multiple_of(at, rows), rows), :size] = piece[side] * (1.0 / (N_ROW * N_COL * edge))
    work[:, size:] = products[...].T
    set_stage(work, stage, 0)

    def block(p, carry):
        eliminate([stage[i * SUB : (i + 1) * SUB, :] for i in range(BLOCK // SUB)], done)
        for q in range(size // BLOCK):
            pl.when(p == q)(lambda q=q: apply_block(work, stage, done, factor, q * BLOCK))
        return carry

    lax.fori_loop(0, size // BLOCK, block, 0)
    basis[...] = work[:, size:].T


def factor_and_basis(table, pieces, products):
    edge, size = products.shape
    vmem = pl.BlockSpec(memory_space=pltpu.VMEM)
    return pl.pallas_call(
        factor_kernel,
        out_shape=(jax.ShapeDtypeStruct((edge, size), F32), jax.ShapeDtypeStruct((size, size), F32)),
        in_specs=[pl.BlockSpec(memory_space=pltpu.SMEM)] + [vmem] * 5,
        out_specs=(vmem, vmem),
        scratch_shapes=[pltpu.VMEM((size, size + edge), F32)] + [pltpu.VMEM((BLOCK, LANES), F32)] * 2,
        compiler_params=pltpu.CompilerParams(vmem_limit_bytes=8 << 20),
        name="factor",
    )(table, *pieces, products)


def gram_pieces(products, r, c):
    width = products.shape[1]
    half, piece = width // N_CORE, width // (N_CORE * N_Y)
    my_core, my_y = r & (N_CORE - 1), c & (N_Y - 1)
    local = jnp.dot(products.T, products, precision=lax.Precision.HIGHEST, preferred_element_type=F32)
    mine = lax.dynamic_slice_in_dim(local, my_core * half, half, 0)
    other = lax.dynamic_slice_in_dim(local, (1 - my_core) * half, half, 0)
    pair = mine + to_core(other)
    parts = [lax.dynamic_slice_in_dim(pair, ((my_y + k) & (N_Y - 1)) * piece, piece, 0) for k in range(N_Y)]
    got = ring_sum([parts[0]] + [to_y(parts[k], k) for k in range(1, N_Y)])
    got = ring_sum([got] + [to_x(got, k) for k in range(1, N_X)])
    got = got + to_zl(got)
    got = ring_sum([got] + [to_z(got, k) for k in range(1, N_ZH)])
    both = jnp.stack([got, to_core(got)])
    return [both] + [to_y(both, -k) for k in range(1, N_Y)]


def body(blocks, block_rows, block_cols, counts, trials):
    edge, width = trials.shape
    r, c = lax.axis_index("row").astype(jnp.int32), lax.axis_index("col").astype(jnp.int32)
    slots = block_rows.shape[1]
    at = lax.broadcasted_iota(jnp.int32, (1, slots), 1)
    table = jnp.concatenate(
        [block_rows, block_cols, jnp.broadcast_to(counts, (1, slots)), jnp.where(at == 0, r, c)], 0
    )
    first = jnp.stack([trials, to_zl(trials)])
    zs = jnp.stack([trials] + [to_z(trials, -k) for k in range(1, N_ZH)])
    row_pieces = [first] + [to_y(first, -k) for k in range(1, N_Y)]
    col_pieces = [zs] + [to_x(zs, -k) for k in range(1, N_X)]
    outs = products_of(
        mirror_kernel,
        table,
        blocks[0],
        row_pieces,
        ([(2 * N_ZH * FIRST + N_X * N_ZH * (edge - FIRST),)] + [(N_ZH, FIRST)] * 2) * N_CORE,
    )
    keep, send = dict(zip((0, 1, 3), outs[:3])), dict(zip((0, 1, 3), outs[3:]))
    col_pieces = col_pieces + [to_core(v) for v in col_pieces]
    row_outs = products_of(direct_kernel, table, blocks[0], col_pieces, [(N_ZL, edge)] * N_Y)
    theirs = {k: to_core(send[k]) for k in (1, 3)}
    theirs[0] = to_core(send[0])
    cut = N_ZH * FIRST
    pair = {k: keep[k] + theirs[k] for k in (1, 3)}
    pair[2] = (keep[0][:cut] + theirs[0][:cut]).reshape(N_ZH, FIRST, width)
    sent = {k: to_x(pair[k], k) for k in (1, 3, 2)}
    own = (keep[0][cut : 2 * cut] + theirs[0][cut : 2 * cut]).reshape(N_ZH, FIRST, width)
    got = ring_sum([own] + [sent[k] for k in range(1, N_X)])
    both = (keep[0][2 * cut :] + theirs[0][2 * cut :]).reshape(N_X * N_ZH, edge - FIRST, width)
    parts = [both[k * N_X : (k + 1) * N_X] for k in range(N_ZH)]
    got_b = ring_sum([parts[0]] + [to_z(parts[k], k) for k in range(1, N_ZH)])
    rows = ring_sum([row_outs[0]] + [to_y(row_outs[k], k) for k in range(1, N_Y)])
    row_sum = rows[0] + to_zl(rows[1])
    sum_b = ring_sum([got_b[0]] + [to_x(got_b[k], k) for k in range(1, N_X)])
    sum_a = ring_sum([got[0]] + [to_z(got[k], k) for k in range(1, N_ZH)])
    col_sum = jnp.concatenate([sum_a, sum_b], 0)
    products = row_sum + col_sum
    return factor_and_basis(table, gram_pieces(products, r, c), products)


def solution(mesh):
    return jax.shard_map(
        body,
        mesh=mesh,
        in_specs=(
            P("row", "col", None, None),
            P("row", "col"),
            P("row", "col"),
            P("row", "col"),
            P(("col", "row"), None),
        ),
        out_specs=(P(("col", "row"), None), P()),
        check_vma=False,
    )
```
